256 devices in a mesh: chan: 64 (over z, y, core), tm: 4 (over x).
Axes of the slice: x: 4, y: 4, z: 8, core: 2. Of those that a mesh axis runs over, the one named last changes fastest.
Arguments:
- traces: float32 [5120, 8192], P('chan', 'tm'), may hold values from -6 to 6
- fir_taps: float32 [65], replicated, may hold values from -0.75 to 0.75
- source_index: int32 [64], replicated, may hold values from 0 to 5119, as said below
Outputs:
- correlation: float32 [4, 64, 5120, 512], P('tm', None, 'chan')
The draws below stay inside these ranges and needn't reach their ends.
Inputs may be any that keep to these rules, and one draw needn't show every extreme that they name: `source_index`: the 64 channel numbers are distinct. They lie in 8 consecutive blocks of 80 channels (block b holding channels b * 80 to b * 80 + 79, counted around the fibre's end), at most 12 in one block, and exactly 12 in some block. Channels 0 and 5119 are always among them.
All inputs are finite; a program needn't handle non-finite values.
Results may differ from the reference program's by a relative error of at most 0.0029.
Values may be sent and summed in bfloat16 or wider, within the bound.
A program may use at most 192 MiB of HBM per device.

```python
import math
import jax
import jax.numpy as jnp
import numpy as np
from jax import lax

CH = 80
T_DEV = 2048
LAG_HALF = 256
FIR_HALF = 32
NORM_HALF = 64
FIR_TAPS = 65
NCH = 5120
NT = 8192
N_TM = 4


def draw_source_index(key, part):
    block_total = NCH // CH
    counts = np.array([12, 12, 10, 8, 8, 6, 4, 4])
    starts = jnp.array(np.concatenate([[0], np.cumsum(counts)[:-1]]), jnp.int32)
    start_key, perm_key, order_key = jax.random.split(key, 3)
    first = jax.random.randint(start_key, (), block_total - 7, block_total)
    block_of = (first + jnp.arange(8)) % block_total
    within = jax.vmap(lambda k: jax.random.permutation(k, CH))(jax.random.split(perm_key, 8))
    target = jnp.where(block_of == 0, 0, CH - 1).astype(jnp.int32)
    forced = (block_of == 0) | (block_of == block_total - 1)
    column = jnp.arange(CH)[None, :]
    leading = within[:, :1]
    swapped = jnp.where(within == target[:, None], leading, jnp.where(column == 0, target[:, None], within))
    within = jnp.where(forced[:, None], swapped, within)
    number = jnp.arange(64)
    rank_of = jnp.sum((number[:, None] >= starts[None, 1:]).astype(jnp.int32), axis=1)
    place = number - starts[rank_of]
    channel = block_of[rank_of] * CH + within[rank_of, place]
    order = jax.random.permutation(order_key, 64)
    return channel[order].astype(jnp.int32)


def block_scale(own_key, dims, shards, least, largest):
    loudness, own = 1.0, jax.random.fold_in(own_key, 6)
    for position, shards_of in shards:
        heights = jnp.exp(jax.random.uniform(jax.random.fold_in(own, position), (shards_of,), jnp.float32, least / len(shards), largest / len(shards)))
        loudness = loudness * jnp.repeat(heights, dims[position] // shards_of).reshape([-1 if axis == position else 1 for axis in range(len(dims))])
    return loudness


def normal_values(own_key, extent, width, limit, cuts=(), kind=jnp.bfloat16):
    entries = jax.random.normal(own_key, extent, jnp.float32) * width
    if len(cuts) > 0:
        entries = block_scale(own_key, extent, cuts, -0.22, 0.18) * entries
    return jnp.clip(entries, min=-limit, max=limit).astype(kind)


def setup_inputs(seed: int = 0) -> dict:
    keys = jax.random.split(jax.random.key(seed), 4)
    return {
        "traces": normal_values(keys[0], (NCH, NT), 1.0, 6.0, ((0, 64), (1, 4)), jnp.float32),
        "fir_taps": normal_values(keys[1], (FIR_TAPS,), FIR_TAPS ** -0.5, 0.75, (), jnp.float32),
        "source_index": draw_source_index(jax.random.fold_in(keys[3], 71), 0),
    }


EPSILON = 1e-05

def bandpass(padded, fir_taps):
    result = lax.conv_general_dilated(padded[:, None, :], fir_taps[None, None, :], (1,), 'VALID', dimension_numbers=('NCH', 'OIH', 'NCH'), precision=lax.Precision.HIGHEST)
    return result[:, 0, :]

def reference(traces, fir_taps, source_index):
    padded = jnp.pad(traces, ((0, 0), (FIR_HALF, FIR_HALF)))
    filtered = bandpass(padded, fir_taps)
    filtered_wide = jnp.pad(filtered, ((0, 0), (NORM_HALF, NORM_HALF)))
    window_sum = lax.reduce_window(jnp.abs(filtered_wide), jnp.zeros((), filtered_wide.dtype), lax.add, (1, 2 * NORM_HALF + 1), (1, 1), 'VALID')
    normed = (filtered / (EPSILON + window_sum / (2 * NORM_HALF + 1))).astype(jnp.bfloat16)
    sources = jnp.take(normed, source_index, axis=0).astype(jnp.float32)
    source_pad = jnp.pad(sources, ((0, 0), (LAG_HALF, LAG_HALF)))
    lag_width = min(128, 2 * LAG_HALF)
    slab_results = []
    for g in range(N_TM):
        window = source_pad[:, g * T_DEV:g * T_DEV + T_DEV + 2 * LAG_HALF]
        receivers = normed[:, g * T_DEV:(g + 1) * T_DEV].astype(jnp.float32)
        pieces = []
        for i in range(2 * LAG_HALF // lag_width):
            hankel = jnp.stack([window[:, i * lag_width + j:i * lag_width + j + T_DEV] for j in range(lag_width)], axis=1)
            pieces.append(jnp.einsum('sjt,ct->scj', hankel, receivers, precision=lax.Precision.HIGHEST))
        slab_results.append(jnp.concatenate(pieces, axis=2) / math.sqrt(T_DEV))
    return jnp.stack(slab_results, axis=0)
```

```python
import math

import jax
import jax.numpy as jnp
from jax import lax
from jax.experimental import pallas as pl
from jax.experimental.pallas import tpu as pltpu
from jax.sharding import Mesh
from jax.sharding import PartitionSpec as P

CHN, T, S = 80, 2048, 64
EPSILON = 1e-05
FIR_HALF, NORM_HALF, LAG_HALF = 32, 64, 256
TAPS = 2 * FIR_HALF + 1
SLOTS = 12
NB = T // 128
NP = T // 256
K = T + 128
AXES = ("chan_0", "chan_1", "chan_2", "tm")
NZ, NY, NC, NX = 8, 4, 2, 4
CHUNKS = ((0, 48), (48, 48), (96, 32))
UP = (True, False, True)
ROWS = 128
BF = jnp.bfloat16
F32 = jnp.float32


def dot(a, b):
    return jnp.dot(a, b, preferred_element_type=F32)


def dot_t(a, b):
    return lax.dot_general(a, b, (((1,), (1,)), ((), ())), preferred_element_type=F32)


def iota(shape, dim):
    return lax.broadcasted_iota(jnp.int32, shape, dim)


def gather_kernel(
    traces, fir, index, src_out, nr_out,
    xbuf, halo, xh, xl, band, fbuf, fa, fb, nb, nrev, pick, edge, pack, zu, zd, gath, unp,
    lsem, hsem, esem, zsem, ysem, csem,
):
    z, y, core, x = (lax.axis_index(a) for a in AXES)
    up_z = {"chan_0": lax.rem(z + 1, NZ)}
    dn_z = {"chan_0": lax.rem(z + NZ - 1, NZ)}
    up_y = {"chan_1": lax.rem(y + 1, NY)}
    dn_y = {"chan_1": lax.rem(y + NY - 1, NY)}
    other = {"chan_2": 1 - core}
    right = {"tm": lax.rem(x + 1, NX)}
    left = {"tm": lax.rem(x + NX - 1, NX)}

    load = pltpu.make_async_copy(traces, xbuf, lsem.at[0])
    load.start()
    barrier = pltpu.get_barrier_semaphore()
    peers = (up_z, dn_z, up_y, dn_y, other, right, left)
    for peer in peers:
        pl.semaphore_signal(barrier, inc=1, device_id=peer, device_id_type=pl.DeviceIdType.MESH)
    pl.semaphore_wait(barrier, len(peers))

    def remote(src, dst, sems, peer):
        return pltpu.make_async_remote_copy(
            src_ref=src, dst_ref=dst, send_sem=sems.at[0], recv_sem=sems.at[1],
            device_id=peer, device_id_type=pl.DeviceIdType.MESH,
        )

    to_right = remote(traces.at[:, T - 128:T], halo.at[0], hsem.at[0], right)
    to_left = remote(traces.at[:, 0:128], halo.at[1], hsem.at[1], left)
    to_right.start()
    to_left.start()

    lane = iota((8, 128), 1)
    taps = jnp.zeros((8, 128), F32)
    for k in range(TAPS):
        taps = jnp.where(lane == k, fir[k], taps)
    rolled = pltpu.roll(jnp.concatenate([taps] * 16, axis=0), 128 - FIR_HALF, 1, stride=1, stride_axis=0)
    apart = iota((128, 128), 1) - iota((128, 128), 0)
    zero = jnp.zeros((128, 128), F32)
    d1 = jnp.where(apart >= 128 - FIR_HALF, rolled, zero)
    d2 = jnp.where(jnp.abs(apart) <= FIR_HALF, rolled, zero)
    d3 = jnp.where(apart <= FIR_HALF - 128, rolled, zero)
    for n, blocks in enumerate((((d1, d2), (zero, d1)), ((d3, zero), (d2, d3)))):
        for i in range(2):
            for u in range(2):
                whole = blocks[i][u]
                high = whole.astype(BF)
                at = (slice(i * 128, i * 128 + 128), slice(u * 128, u * 128 + 128))
                band[(2 * n,) + at] = high
                band[(2 * n + 1,) + at] = (whole - high.astype(F32)).astype(BF)
    gap = iota((256, 256), 0) - iota((256, 256), 1)
    one = jnp.ones((256, 256), F32)
    none = jnp.zeros((256, 256), F32)
    band[4] = jnp.where((gap >= NORM_HALF) & (gap <= 3 * NORM_HALF), one, none).astype(BF)
    band[5] = jnp.where((gap <= -NORM_HALF) & (gap >= -3 * NORM_HALF), one, none).astype(BF)
    band[6] = jnp.where(iota((256, 256), 0) + iota((256, 256), 1) == 255, one, none).astype(BF)

    own = (z * NY + y) * NC + core
    lanes = iota((128, 128), 1)
    subs = iota((128, 128), 0)
    row = jnp.full((8, 128), -1, jnp.int32)
    for s in range(S):
        row = jnp.where(lane == s, index[s], row)
    rows = jnp.concatenate([row] * 16, axis=0)
    inside = (rows >= own * CHN) & (rows < own * CHN + CHN)
    fone, fnone = jnp.ones((128, 128), F32), jnp.zeros((128, 128), F32)
    mine = jnp.where(inside, fone, fnone)
    before = jnp.where(subs < lanes, fone, fnone)
    rank = dot(mine.astype(BF), before.astype(BF))
    hit = jnp.where(inside & (rows == own * CHN + subs), fone, fnone).astype(BF)[0:CHN]
    subf = subs.astype(F32)
    for i in range(4):
        slot = jnp.where(inside & (subf == rank + SLOTS * i), fone, fnone).astype(BF)[0:48]
        pick[i] = dot_t(slot, hit).astype(BF)

    colsum = jnp.sum(jnp.where(subs == lanes, rows.astype(F32), fnone), axis=1, keepdims=True)
    owner_col = jnp.floor((colsum + 0.5) * (1.0 / CHN))
    owner_row = jnp.floor((rows.astype(F32) + 0.5) * (1.0 / CHN))
    rank_col = jnp.sum(
        jnp.where((owner_row == owner_col) & (lanes < subs), fone, fnone), axis=1, keepdims=True
    )
    residue = owner_col - 8.0 * jnp.floor(owner_col * 0.125)
    place = (residue * ROWS + rank_col)[0:S]
    wide = iota((S, 8 * ROWS), 1).astype(F32)
    uone, unone = jnp.ones((S, 8 * ROWS), F32), jnp.zeros((S, 8 * ROWS), F32)
    for e in range(NP + 2):
        offset = 96 if e == 0 else 112 if e == NP + 1 else SLOTS * (e - 1)
        unp[e * S:(e + 1) * S, :] = jnp.where(wide == place + offset, uone, unone).astype(BF)

    def put(group, half, block):
        high = block.astype(BF)
        at = (slice(group * CHN, group * CHN + CHN), slice(half * 128, half * 128 + 128))
        xh[at] = high
        xl[at] = (block - high.astype(F32)).astype(BF)

    load.wait()
    for b in range(NB):
        put(1 + b // 2, b % 2, xbuf[:, b * 128:b * 128 + 128])
    nothing = jnp.zeros((CHN, 128), F32)
    put(0, 0, nothing)
    put(NP + 1, 1, nothing)

    def filtered(lo, hi):
        n = slice(lo * CHN, hi * CHN)
        m = slice((lo + 1) * CHN, (hi + 1) * CHN)
        value = dot_t(xh[n], band[0]) + dot_t(xh[m], band[2])
        value += dot_t(xl[n], band[0]) + dot_t(xl[m], band[2])
        value += dot_t(xh[n], band[1]) + dot_t(xh[m], band[3])
        return value

    def keep(lo, hi, value):
        n = slice(lo * CHN, hi * CHN)
        fbuf[n] = value
        size = jnp.abs(value)
        high = size.astype(BF)
        fa[n] = high
        fb[n] = (size - high.astype(F32)).astype(BF)

    keep(1, NP, filtered(1, NP))
    to_right.wait_recv()
    to_left.wait_recv()
    put(0, 1, jnp.where(x > 0, halo[0], nothing))
    put(NP + 1, 0, jnp.where(x < NX - 1, halo[1], nothing))
    ends = iota((CHN, 256), 1)
    empty = jnp.zeros((CHN, 256), F32)
    keep(0, 1, jnp.where((ends >= 128) | (x > 0), filtered(0, 1), empty))
    keep(NP, NP + 1, jnp.where((ends < 128) | (x < NX - 1), filtered(NP, NP + 1), empty))

    first, second = slice(0, NP * CHN), slice(CHN, (NP + 1) * CHN)
    level = dot(fa[first], band[4]) + dot(fa[second], band[5])
    level += dot(fb[first], band[4]) + dot(fb[second], band[5])
    below = EPSILON + level / (2 * NORM_HALF + 1)
    nb[:, 0:128] = (fbuf[first, 128:256] / below[:, 0:128]).astype(BF)
    nb[:, 128:256] = (fbuf[second, 0:128] / below[:, 128:256]).astype(BF)

    def pair(p):
        return nb[p * CHN:(p + 1) * CHN]

    lower = dot(pick[0], pair(0))[0:16]
    upper = dot(pick[0], pair(NP - 1))[0:16]
    edge[0] = jnp.where(x > 0, lower, jnp.zeros_like(lower)).astype(BF)
    edge[1] = jnp.where(x < NX - 1, upper, jnp.zeros_like(upper)).astype(BF)
    for j in range(2):
        total = dot(pick[0], pair(4 * j))
        for i in range(1, 4):
            total += dot(pick[i], pair(4 * j + i))
        pack[48 * j:48 * j + 48, :] = total.astype(BF)

    edge_left = remote(edge.at[0], pack.at[112:128], esem.at[0], left)
    edge_right = remote(edge.at[1], pack.at[96:112], esem.at[1], right)
    edge_left.start()
    edge_right.start()

    def part(ref, k):
        at, size = CHUNKS[k]
        return ref.at[at:at + size]

    def ring(direction, hop, k):
        slots, peer = (zu, up_z) if direction == 0 else (zd, dn_z)
        src = part(pack, k) if hop == 0 else part(slots.at[hop - 1], k)
        return remote(src, part(slots.at[hop], k), zsem.at[direction, hop, k], peer)

    def rings(hop, k):
        return [d for d in range(2) if hop < 3 or (d == 0) == UP[k]]

    started = [to_right, to_left, edge_left, edge_right]

    def go(copy):
        copy.start()
        started.append(copy)

    for k in range(2):
        for d in rings(0, k):
            go(ring(d, 0, k))
    edge_left.wait_recv()
    edge_right.wait_recv()
    for d in rings(0, 2):
        go(ring(d, 0, 2))

    turned = dot(nb[...], band[6])
    for p in range(NP):
        for h in range(2):
            nrev[(NP - 1 - p) * 2 + h] = turned[p * CHN:(p + 1) * CHN, h * 128:h * 128 + 128]
    save = pltpu.make_async_copy(nrev, nr_out, lsem.at[1])
    save.start()

    for hop in range(1, 4):
        for k in range(3):
            for d in range(2):
                ring(d, hop - 1, k).wait_recv()
                if d in rings(hop, k):
                    go(ring(d, hop, k))

    me = y * NC + core

    def hold(slot, k):
        at, size = CHUNKS[k]
        return gath.at[slot, at:at + size]

    low, high = lax.rem(y + NY - 1, NY) * NC + core, lax.rem(y + 1, NY) * NC + core
    far = lax.rem(y + 2, NY) * NC + core
    origin = (me, low, high, far)

    def line(kind, k):
        if kind == 0:
            slot, peer = me, up_y
        elif kind == 1:
            slot, peer = me, dn_y
        else:
            slot, peer = (low, up_y) if UP[k] else (high, dn_y)
        return remote(hold(slot, k), hold(slot, k), ysem.at[kind, k], peer)

    def across(n, k):
        return remote(hold(origin[n], k), hold(origin[n], k), csem.at[n, k], other)

    for k in range(3):
        at, size = CHUNKS[k]
        for d in rings(3, k):
            ring(d, 3, k).wait_recv()
        total = pack[at:at + size]
        for hop in range(3):
            total += zu[hop, at:at + size] + zd[hop, at:at + size]
        total += (zu if UP[k] else zd)[3, at:at + size]
        gath[me, at:at + size] = total
        go(line(0, k))
        go(line(1, k))
        go(across(0, k))
    for k in range(3):
        line(0, k).wait_recv()
        if UP[k]:
            go(line(2, k))
        go(across(1, k))
        line(1, k).wait_recv()
        if not UP[k]:
            go(line(2, k))
        go(across(2, k))
    for k in range(3):
        line(2, k).wait_recv()
        go(across(3, k))
    for n in range(4):
        for k in range(3):
            across(n, k).wait_recv()

    spread = dot(unp[...], gath[...].reshape(8 * ROWS, 256)).astype(BF)
    for e in range(NP + 2):
        src_out[:, e * 256:(e + 1) * 256] = spread[e * S:(e + 1) * S]
    for copy in started:
        copy.wait_send()
    save.wait()


def gather(traces, fir, index):
    dma = pltpu.SemaphoreType.DMA
    return pl.pallas_call(
        gather_kernel,
        in_specs=[
            pl.BlockSpec(memory_space=pl.ANY),
            pl.BlockSpec(memory_space=pltpu.SMEM),
            pl.BlockSpec(memory_space=pltpu.SMEM),
        ],
        out_specs=[pl.BlockSpec(memory_space=pltpu.VMEM), pl.BlockSpec(memory_space=pl.ANY)],
        out_shape=[
            jax.ShapeDtypeStruct((S, T + 2 * LAG_HALF), BF),
            jax.ShapeDtypeStruct((NB, CHN, 128), F32),
        ],
        scratch_shapes=[
            pltpu.VMEM((CHN, T), F32),
            pltpu.VMEM((2, CHN, 128), F32),
            pltpu.VMEM(((NP + 2) * CHN, 256), BF),
            pltpu.VMEM(((NP + 2) * CHN, 256), BF),
            pltpu.VMEM((7, 256, 256), BF),
            pltpu.VMEM(((NP + 1) * CHN, 256), F32),
            pltpu.VMEM(((NP + 1) * CHN, 256), BF),
            pltpu.VMEM(((NP + 1) * CHN, 256), BF),
            pltpu.VMEM((NP * CHN, 256), BF),
            pltpu.VMEM((NB, CHN, 128), F32),
            pltpu.VMEM((4, 48, CHN), BF),
            pltpu.VMEM((2, 16, 256), BF),
            pltpu.VMEM((ROWS, 256), BF),
            pltpu.VMEM((4, ROWS, 256), BF),
            pltpu.VMEM((4, ROWS, 256), BF),
            pltpu.VMEM((8, ROWS, 256), BF),
            pltpu.VMEM(((NP + 2) * S, 8 * ROWS), BF),
            dma((2,)),
            dma((2, 2)),
            dma((2, 2)),
            dma((2, 4, 3, 2)),
            dma((3, 3, 2)),
            dma((4, 3, 2)),
        ],
        compiler_params=pltpu.CompilerParams(
            collective_id=0, has_side_effects=True, vmem_limit_bytes=40 << 20
        ),
        name="gather",
    )(traces, fir, index)


def corr_kernel(src_ref, nr_ref, o_ref, w_ref, h0, h1):
    g = pl.program_id(0)
    keep = iota((128, 128), 1) > iota((128, 128), 0)

    def build(h, c, half):
        cols = slice(half * 128, half * 128 + 128)
        prev = jnp.zeros((128, 128), F32)
        for q in range(NB + 1):
            b = NB - q
            if b >= 1:
                x = nr_ref.at[b - 1][pl.ds(c, 128, stride=0), :]
                cur = pltpu.roll(x, 1, 1, stride=1, stride_axis=0)
            else:
                cur = jnp.zeros((128, 128), F32)
            h[q * 128:(q + 1) * 128, cols] = jnp.where(keep, prev, cur).astype(BF)
            prev = cur

    @pl.when(g == 0)
    def _():
        for a in range(4):
            w_ref[a * S:(a + 1) * S, :] = src_ref[:, a * 128:a * 128 + K]
        build(h0, 0, 0)
        build(h0, 1, 1)

    out2 = o_ref.reshape(S * 4 * 8, 128)
    bufs = (h0, h1)
    for p in range(4):
        nxt = lax.rem(g * 8 + 2 * p + 2, CHN)
        build(bufs[(p + 1) % 2], nxt, 0)
        build(bufs[(p + 1) % 2], nxt + 1, 1)
        res = dot(w_ref[...], bufs[p % 2][...]) * (1.0 / math.sqrt(T))
        for a in range(4):
            for hh in range(2):
                out2[pl.ds(a * 8 + 2 * p + hh, S, stride=32), :] = res[
                    a * S:(a + 1) * S, hh * 128:hh * 128 + 128
                ]


def corr(src_ext, nr):
    out = pl.pallas_call(
        corr_kernel,
        grid=(CHN // 8,),
        in_specs=[
            pl.BlockSpec((S, T + 2 * LAG_HALF), lambda g: (0, 0)),
            pl.BlockSpec((NB, CHN, 128), lambda g: (0, 0, 0)),
        ],
        out_specs=pl.BlockSpec((S, 1, 4, 8, 128), lambda g: (0, g, 0, 0, 0)),
        out_shape=jax.ShapeDtypeStruct((S, CHN // 8, 4, 8, 128), F32),
        scratch_shapes=[
            pltpu.VMEM((4 * S, K), BF),
            pltpu.VMEM((K, 256), BF),
            pltpu.VMEM((K, 256), BF),
        ],
        compiler_params=pltpu.CompilerParams(
            dimension_semantics=("arbitrary",), vmem_limit_bytes=60 << 20
        ),
        name="corr",
    )(src_ext, nr)
    return out.transpose(0, 1, 3, 2, 4).reshape(S, CHN, 2 * LAG_HALF)


def body(traces, fir_taps, source_index):
    src_ext, nr = gather(traces, fir_taps, source_index)
    return corr(src_ext, nr)[None]


def solution(mesh):
    torus = Mesh(mesh.devices.reshape(NZ, NY, NC, NX), AXES)
    chan = AXES[:3]
    return jax.shard_map(
        body,
        mesh=torus,
        in_specs=(P(chan, "tm"), P(), P()),
        out_specs=P("tm", None, chan, None),
        check_vma=False,
    )
```

```python
import math

import jax
import jax.numpy as jnp
from jax import lax
from jax.experimental import pallas as pl
from jax.experimental.pallas import tpu as pltpu
from jax.sharding import Mesh
from jax.sharding import PartitionSpec as P

CHN, T, S = 80, 2048, 64
EPSILON = 1e-05
FIR_HALF, NORM_HALF, LAG_HALF = 32, 64, 256
TAPS = 2 * FIR_HALF + 1
SLOTS = 12
NB = T // 128
NP = T // 256
K = T + 128
AXES = ("chan_0", "chan_1", "chan_2", "tm")
NZ, NY, NC, NX = 8, 4, 2, 4
CHUNKS = ((0, 48), (48, 48), (96, 32))
UP = (True, False, True)
ROWS = 128
ORDER = (1, 2, 3, 4, 5, 6, 0, 7)
BF = jnp.bfloat16
F32 = jnp.float32


def dot(a, b):
    return jnp.dot(a, b, preferred_element_type=F32)


def dot_t(a, b):
    return lax.dot_general(a, b, (((1,), (1,)), ((), ())), preferred_element_type=F32)


def iota(shape, dim):
    return lax.broadcasted_iota(jnp.int32, shape, dim)


def gather_kernel(
    traces, fir, index, src_out, nr_out,
    xbuf, halo, xh, xl, band, fbuf, fa, fb, nb, nrev, pick, edge, pack, zu, zd, gath, unp,
    lsem, hsem, esem, zsem, ysem, csem,
):
    z, y, core, x = (lax.axis_index(a) for a in AXES)
    up_z = {"chan_0": lax.rem(z + 1, NZ)}
    dn_z = {"chan_0": lax.rem(z + NZ - 1, NZ)}
    up2_z = {"chan_0": lax.rem(z + 2, NZ)}
    dn2_z = {"chan_0": lax.rem(z + NZ - 2, NZ)}
    up_y = {"chan_1": lax.rem(y + 1, NY)}
    dn_y = {"chan_1": lax.rem(y + NY - 1, NY)}
    far_y = {"chan_1": lax.rem(y + 2, NY)}
    other = {"chan_2": 1 - core}
    right = {"tm": lax.rem(x + 1, NX)}
    left = {"tm": lax.rem(x + NX - 1, NX)}

    load = pltpu.make_async_copy(traces, xbuf, lsem.at[0])
    load.start()
    barrier = pltpu.get_barrier_semaphore()
    peers = (up2_z, dn2_z, up_z, dn_z, far_y, up_y, dn_y, other, right, left)
    for peer in peers:
        pl.semaphore_signal(barrier, inc=1, device_id=peer, device_id_type=pl.DeviceIdType.MESH)
    pl.semaphore_wait(barrier, len(peers))

    def remote(src, dst, sems, peer):
        return pltpu.make_async_remote_copy(
            src_ref=src, dst_ref=dst, send_sem=sems.at[0], recv_sem=sems.at[1],
            device_id=peer, device_id_type=pl.DeviceIdType.MESH,
        )

    to_right = remote(traces.at[:, T - 128:T], halo.at[0], hsem.at[0], right)
    to_left = remote(traces.at[:, 0:128], halo.at[1], hsem.at[1], left)
    to_right.start()
    to_left.start()

    lane = iota((8, 128), 1)
    taps = jnp.zeros((8, 128), F32)
    for k in range(TAPS):
        taps = jnp.where(lane == k, fir[k], taps)
    rolled = pltpu.roll(jnp.concatenate([taps] * 16, axis=0), 128 - FIR_HALF, 1, stride=1, stride_axis=0)
    apart = iota((128, 128), 1) - iota((128, 128), 0)
    zero = jnp.zeros((128, 128), F32)
    d1 = jnp.where(apart >= 128 - FIR_HALF, rolled, zero)
    d2 = jnp.where(jnp.abs(apart) <= FIR_HALF, rolled, zero)
    d3 = jnp.where(apart <= FIR_HALF - 128, rolled, zero)
    for n, blocks in enumerate((((d1, d2), (zero, d1)), ((d3, zero), (d2, d3)))):
        for i in range(2):
            for u in range(2):
                whole = blocks[i][u]
                high = whole.astype(BF)
                at = (slice(i * 128, i * 128 + 128), slice(u * 128, u * 128 + 128))
                band[(2 * n,) + at] = high
                band[(2 * n + 1,) + at] = (whole - high.astype(F32)).astype(BF)
    gap = iota((256, 256), 0) - iota((256, 256), 1)
    one = jnp.ones((256, 256), F32)
    none = jnp.zeros((256, 256), F32)
    band[4] = jnp.where((gap >= NORM_HALF) & (gap <= 3 * NORM_HALF), one, none).astype(BF)
    band[5] = jnp.where((gap <= -NORM_HALF) & (gap >= -3 * NORM_HALF), one, none).astype(BF)
    band[6] = jnp.where(iota((256, 256), 0) + iota((256, 256), 1) == 255, one, none).astype(BF)

    own = (z * NY + y) * NC + core
    lanes = iota((128, 128), 1)
    subs = iota((128, 128), 0)
    row = jnp.full((8, 128), -1, jnp.int32)
    for s in range(S):
        row = jnp.where(lane == s, index[s], row)
    rows = jnp.concatenate([row] * 16, axis=0)
    inside = (rows >= own * CHN) & (rows < own * CHN + CHN)
    fone, fnone = jnp.ones((128, 128), F32), jnp.zeros((128, 128), F32)
    mine = jnp.where(inside, fone, fnone)
    before = jnp.where(subs < lanes, fone, fnone)
    rank = dot(mine.astype(BF), before.astype(BF))
    hit = jnp.where(inside & (rows == own * CHN + subs), fone, fnone).astype(BF)[0:CHN]
    subf = subs.astype(F32)
    for i in range(4):
        slot = jnp.where(inside & (subf == rank + SLOTS * i), fone, fnone).astype(BF)[0:48]
        pick[i] = dot_t(slot, hit).astype(BF)

    colsum = jnp.sum(jnp.where(subs == lanes, rows.astype(F32), fnone), axis=1, keepdims=True)
    owner_col = jnp.floor((colsum + 0.5) * (1.0 / CHN))
    owner_row = jnp.floor((rows.astype(F32) + 0.5) * (1.0 / CHN))
    rank_col = jnp.sum(
        jnp.where((owner_row == owner_col) & (lanes < subs), fone, fnone), axis=1, keepdims=True
    )
    residue = owner_col - 8.0 * jnp.floor(owner_col * 0.125)
    place = (residue * ROWS + rank_col)[0:S]
    wide = iota((S, 8 * ROWS), 1).astype(F32)
    uone, unone = jnp.ones((S, 8 * ROWS), F32), jnp.zeros((S, 8 * ROWS), F32)
    for e in range(NP + 2):
        offset = 96 if e == 0 else 112 if e == NP + 1 else SLOTS * ORDER.index(e - 1)
        unp[e * S:(e + 1) * S, :] = jnp.where(wide == place + offset, uone, unone).astype(BF)

    def put(group, half, block):
        high = block.astype(BF)
        at = (slice(group * CHN, group * CHN + CHN), slice(half * 128, half * 128 + 128))
        xh[at] = high
        xl[at] = (block - high.astype(F32)).astype(BF)

    load.wait()
    for b in range(NB):
        put(1 + b // 2, b % 2, xbuf[:, b * 128:b * 128 + 128])
    nothing = jnp.zeros((CHN, 128), F32)
    put(0, 0, nothing)
    put(NP + 1, 1, nothing)

    def filtered(lo, hi):
        n = slice(lo * CHN, hi * CHN)
        m = slice((lo + 1) * CHN, (hi + 1) * CHN)
        value = dot_t(xh[n], band[0]) + dot_t(xh[m], band[2])
        value += dot_t(xl[n], band[0]) + dot_t(xl[m], band[2])
        value += dot_t(xh[n], band[1]) + dot_t(xh[m], band[3])
        return value

    def keep(lo, hi, value):
        n = slice(lo * CHN, hi * CHN)
        fbuf[n] = value
        size = jnp.abs(value)
        high = size.astype(BF)
        fa[n] = high
        fb[n] = (size - high.astype(F32)).astype(BF)

    def normalize(lo, hi):
        first, second = slice(lo * CHN, hi * CHN), slice((lo + 1) * CHN, (hi + 1) * CHN)
        level = dot(fa[first], band[4]) + dot(fa[second], band[5])
        level += dot(fb[first], band[4]) + dot(fb[second], band[5])
        below = EPSILON + level / (2 * NORM_HALF + 1)
        nb[first, 0:128] = (fbuf[first, 128:256] / below[:, 0:128]).astype(BF)
        nb[first, 128:256] = (fbuf[second, 0:128] / below[:, 128:256]).astype(BF)

    def pair(p):
        return nb[p * CHN:(p + 1) * CHN]

    def fold(j):
        total = dot(pick[0], pair(ORDER[4 * j]))
        for i in range(1, 4):
            total += dot(pick[i], pair(ORDER[4 * j + i]))
        pack[48 * j:48 * j + 48, :] = total.astype(BF)

    def part(ref, k):
        at, size = CHUNKS[k]
        return ref.at[at:at + size]

    def ring(d, far, k):
        slots, two, near = (zu, up2_z, up_z) if d == 0 else (zd, dn2_z, dn_z)
        src = part(pack, k) if far < 2 else part(slots.at[1], k)
        peer = (near, two, near, two)[far]
        return remote(src, part(slots.at[far], k), zsem.at[d, far, k], peer)

    def rings(far, k):
        return [d for d in range(2) if far < 3 or (d == 0) == UP[k]]

    started = [to_right, to_left]

    def go(copy):
        copy.start()
        started.append(copy)

    def send(k):
        for far in (1, 0):
            for d in range(2):
                go(ring(d, far, k))

    keep(1, NP, filtered(1, NP))
    normalize(1, NP - 1)
    fold(0)
    send(0)
    to_right.wait_recv()
    to_left.wait_recv()
    put(0, 1, jnp.where(x > 0, halo[0], nothing))
    put(NP + 1, 0, jnp.where(x < NX - 1, halo[1], nothing))
    ends = iota((CHN, 256), 1)
    empty = jnp.zeros((CHN, 256), F32)
    keep(0, 1, jnp.where((ends >= 128) | (x > 0), filtered(0, 1), empty))
    keep(NP, NP + 1, jnp.where((ends < 128) | (x < NX - 1), filtered(NP, NP + 1), empty))
    normalize(0, 1)
    normalize(NP - 1, NP)
    lower = dot(pick[0], pair(0))[0:16]
    upper = dot(pick[0], pair(NP - 1))[0:16]
    edge[0] = jnp.where(x > 0, lower, jnp.zeros_like(lower)).astype(BF)
    edge[1] = jnp.where(x < NX - 1, upper, jnp.zeros_like(upper)).astype(BF)

    edge_left = remote(edge.at[0], pack.at[112:128], esem.at[0], left)
    edge_right = remote(edge.at[1], pack.at[96:112], esem.at[1], right)
    go(edge_left)
    go(edge_right)
    fold(1)
    send(1)
    turned = dot(nb[...], band[6])
    for p in range(NP):
        for h in range(2):
            nrev[(NP - 1 - p) * 2 + h] = turned[p * CHN:(p + 1) * CHN, h * 128:h * 128 + 128]
    save = pltpu.make_async_copy(nrev, nr_out, lsem.at[1])
    save.start()

    def onward(k):
        for d in range(2):
            ring(d, 1, k).wait_recv()
            go(ring(d, 2, k))
            if d in rings(3, k):
                go(ring(d, 3, k))

    onward(0)
    edge_left.wait_recv()
    edge_right.wait_recv()
    send(2)
    onward(1)
    onward(2)

    me = y * NC + core

    def hold(slot, k):
        at, size = CHUNKS[k]
        return gath.at[slot, at:at + size]

    low, high = lax.rem(y + NY - 1, NY) * NC + core, lax.rem(y + 1, NY) * NC + core
    far = lax.rem(y + 2, NY) * NC + core
    origin = (me, low, high, far)

    def line(kind, k):
        return remote(hold(me, k), hold(me, k), ysem.at[kind, k], (up_y, dn_y, far_y)[kind])

    def across(n, k):
        return remote(hold(origin[n], k), hold(origin[n], k), csem.at[n, k], other)

    for k in range(3):
        at, size = CHUNKS[k]
        total = pack[at:at + size]
        for far in (0, 2, 3):
            for d in rings(far, k):
                ring(d, far, k).wait_recv()
        for far in range(3):
            total += zu[far, at:at + size] + zd[far, at:at + size]
        total += (zu if UP[k] else zd)[3, at:at + size]
        gath[me, at:at + size] = total
        for kind in (2, 0, 1):
            go(line(kind, k))
        go(across(0, k))
    for k in range(3):
        for kind in range(3):
            line(kind, k).wait_recv()
            go(across(1 + kind, k))
    for n in range(4):
        for k in range(3):
            across(n, k).wait_recv()

    spread = dot(unp[...], gath[...].reshape(8 * ROWS, 256)).astype(BF)
    for e in range(NP + 2):
        src_out[:, e * 256:(e + 1) * 256] = spread[e * S:(e + 1) * S]
    for copy in started:
        copy.wait_send()
    save.wait()


def gather(traces, fir, index):
    dma = pltpu.SemaphoreType.DMA
    return pl.pallas_call(
        gather_kernel,
        in_specs=[
            pl.BlockSpec(memory_space=pl.ANY),
            pl.BlockSpec(memory_space=pltpu.SMEM),
            pl.BlockSpec(memory_space=pltpu.SMEM),
        ],
        out_specs=[pl.BlockSpec(memory_space=pltpu.VMEM), pl.BlockSpec(memory_space=pl.ANY)],
        out_shape=[
            jax.ShapeDtypeStruct((S, T + 2 * LAG_HALF), BF),
            jax.ShapeDtypeStruct((NB, CHN, 128), F32),
        ],
        scratch_shapes=[
            pltpu.VMEM((CHN, T), F32),
            pltpu.VMEM((2, CHN, 128), F32),
            pltpu.VMEM(((NP + 2) * CHN, 256), BF),
            pltpu.VMEM(((NP + 2) * CHN, 256), BF),
            pltpu.VMEM((7, 256, 256), BF),
            pltpu.VMEM(((NP + 1) * CHN, 256), F32),
            pltpu.VMEM(((NP + 1) * CHN, 256), BF),
            pltpu.VMEM(((NP + 1) * CHN, 256), BF),
            pltpu.VMEM((NP * CHN, 256), BF),
            pltpu.VMEM((NB, CHN, 128), F32),
            pltpu.VMEM((4, 48, CHN), BF),
            pltpu.VMEM((2, 16, 256), BF),
            pltpu.VMEM((ROWS, 256), BF),
            pltpu.VMEM((4, ROWS, 256), BF),
            pltpu.VMEM((4, ROWS, 256), BF),
            pltpu.VMEM((8, ROWS, 256), BF),
            pltpu.VMEM(((NP + 2) * S, 8 * ROWS), BF),
            dma((2,)),
            dma((2, 2)),
            dma((2, 2)),
            dma((2, 4, 3, 2)),
            dma((3, 3, 2)),
            dma((4, 3, 2)),
        ],
        compiler_params=pltpu.CompilerParams(
            collective_id=0, has_side_effects=True, vmem_limit_bytes=63 << 20
        ),
        name="gather",
    )(traces, fir, index)


def corr_kernel(src_ref, nr_ref, o_ref, w_ref, h0, h1):
    g = pl.program_id(0)
    keep = iota((128, 128), 1) > iota((128, 128), 0)

    def build(h, c, half):
        cols = slice(half * 128, half * 128 + 128)
        prev = jnp.zeros((128, 128), F32)
        for q in range(NB + 1):
            b = NB - q
            if b >= 1:
                x = nr_ref.at[b - 1][pl.ds(c, 128, stride=0), :]
                cur = pltpu.roll(x, 1, 1, stride=1, stride_axis=0)
            else:
                cur = jnp.zeros((128, 128), F32)
            h[q * 128:(q + 1) * 128, cols] = jnp.where(keep, prev, cur).astype(BF)
            prev = cur

    @pl.when(g == 0)
    def _():
        for a in range(4):
            w_ref[a * S:(a + 1) * S, :] = src_ref[:, a * 128:a * 128 + K]
        build(h0, 0, 0)
        build(h0, 1, 1)

    out2 = o_ref.reshape(S * 4 * 8, 128)
    bufs = (h0, h1)
    for p in range(4):
        nxt = lax.rem(g * 8 + 2 * p + 2, CHN)
        build(bufs[(p + 1) % 2], nxt, 0)
        build(bufs[(p + 1) % 2], nxt + 1, 1)
        res = dot(w_ref[...], bufs[p % 2][...]) * (1.0 / math.sqrt(T))
        for a in range(4):
            for hh in range(2):
                out2[pl.ds(a * 8 + 2 * p + hh, S, stride=32), :] = res[
                    a * S:(a + 1) * S, hh * 128:hh * 128 + 128
                ]


def corr(src_ext, nr):
    out = pl.pallas_call(
        corr_kernel,
        grid=(CHN // 8,),
        in_specs=[
            pl.BlockSpec((S, T + 2 * LAG_HALF), lambda g: (0, 0)),
            pl.BlockSpec((NB, CHN, 128), lambda g: (0, 0, 0)),
        ],
        out_specs=pl.BlockSpec((S, 1, 4, 8, 128), lambda g: (0, g, 0, 0, 0)),
        out_shape=jax.ShapeDtypeStruct((S, CHN // 8, 4, 8, 128), F32),
        scratch_shapes=[
            pltpu.VMEM((4 * S, K), BF),
            pltpu.VMEM((K, 256), BF),
            pltpu.VMEM((K, 256), BF),
        ],
        compiler_params=pltpu.CompilerParams(
            dimension_semantics=("arbitrary",), vmem_limit_bytes=63 << 20
        ),
        name="corr",
    )(src_ext, nr)
    return out.transpose(0, 1, 3, 2, 4).reshape(S, CHN, 2 * LAG_HALF)


def body(traces, fir_taps, source_index):
    src_ext, nr = gather(traces, fir_taps, source_index)
    return corr(src_ext, nr)[None]


def solution(mesh):
    torus = Mesh(mesh.devices.reshape(NZ, NY, NC, NX), AXES)
    chan = AXES[:3]
    return jax.shard_map(
        body,
        mesh=torus,
        in_specs=(P(chan, "tm"), P(), P()),
        out_specs=P("tm", None, chan, None),
        check_vma=False,
    )
```

```python
import math

import jax
import jax.numpy as jnp
from jax import lax
from jax.experimental import pallas as pl
from jax.experimental.pallas import tpu as pltpu
from jax.sharding import Mesh
from jax.sharding import PartitionSpec as P

CHN, T, S = 80, 2048, 64
EPSILON = 1e-05
FIR_HALF, NORM_HALF, LAG_HALF = 32, 64, 256
TAPS = 2 * FIR_HALF + 1
SLOTS = 12
NB = T // 128
NP = T // 256
KB = NB + 3
K = KB * 128
STEP = 16
WIDE = 2
AXES = ("chan_0", "chan_1", "chan_2", "tm")
NZ, NY, NC, NX = 8, 4, 2, 4
CHUNKS = ((0, 48), (48, 48), (96, 32))
UP = (True, False, True)
ROWS = 128
ORDER = (1, 2, 3, 4, 5, 6, 0, 7)
BF = jnp.bfloat16
F32 = jnp.float32


def dot(a, b):
    return jnp.dot(a, b, preferred_element_type=F32)


def dot_t(a, b):
    return lax.dot_general(a, b, (((1,), (1,)), ((), ())), preferred_element_type=F32)


def iota(shape, dim):
    return lax.broadcasted_iota(jnp.int32, shape, dim)


def gather_kernel(
    traces, fir, index, src_out, nr_out,
    xbuf, halo, xh, xl, band, fbuf, fa, fb, nb, nrev, pick, edge, pack, zu, zd, gath, unp,
    lsem, hsem, esem, zsem, ysem, csem,
):
    z, y, core, x = (lax.axis_index(a) for a in AXES)
    up_z = {"chan_0": lax.rem(z + 1, NZ)}
    dn_z = {"chan_0": lax.rem(z + NZ - 1, NZ)}
    up2_z = {"chan_0": lax.rem(z + 2, NZ)}
    dn2_z = {"chan_0": lax.rem(z + NZ - 2, NZ)}
    up_y = {"chan_1": lax.rem(y + 1, NY)}
    dn_y = {"chan_1": lax.rem(y + NY - 1, NY)}
    far_y = {"chan_1": lax.rem(y + 2, NY)}
    other = {"chan_2": 1 - core}
    right = {"tm": lax.rem(x + 1, NX)}
    left = {"tm": lax.rem(x + NX - 1, NX)}

    load = pltpu.make_async_copy(traces, xbuf, lsem.at[0])
    load.start()
    barrier = pltpu.get_barrier_semaphore()
    peers = (up2_z, dn2_z, up_z, dn_z, far_y, up_y, dn_y, other, right, left)
    for peer in peers:
        pl.semaphore_signal(barrier, inc=1, device_id=peer, device_id_type=pl.DeviceIdType.MESH)
    pl.semaphore_wait(barrier, len(peers))

    def remote(src, dst, sems, peer):
        return pltpu.make_async_remote_copy(
            src_ref=src, dst_ref=dst, send_sem=sems.at[0], recv_sem=sems.at[1],
            device_id=peer, device_id_type=pl.DeviceIdType.MESH,
        )

    to_right = remote(traces.at[:, T - 128:T], halo.at[0], hsem.at[0], right)
    to_left = remote(traces.at[:, 0:128], halo.at[1], hsem.at[1], left)
    to_right.start()
    to_left.start()

    lane = iota((8, 128), 1)
    taps = jnp.zeros((8, 128), F32)
    for k in range(TAPS):
        taps = jnp.where(lane == k, fir[k], taps)
    rolled = pltpu.roll(jnp.concatenate([taps] * 16, axis=0), 128 - FIR_HALF, 1, stride=1, stride_axis=0)
    apart = iota((128, 128), 1) - iota((128, 128), 0)
    zero = jnp.zeros((128, 128), F32)
    d1 = jnp.where(apart >= 128 - FIR_HALF, rolled, zero)
    d2 = jnp.where(jnp.abs(apart) <= FIR_HALF, rolled, zero)
    d3 = jnp.where(apart <= FIR_HALF - 128, rolled, zero)
    for n, blocks in enumerate((((d1, d2), (zero, d1)), ((d3, zero), (d2, d3)))):
        for i in range(2):
            for u in range(2):
                whole = blocks[i][u]
                high = whole.astype(BF)
                at = (slice(i * 128, i * 128 + 128), slice(u * 128, u * 128 + 128))
                band[(2 * n,) + at] = high
                band[(2 * n + 1,) + at] = (whole - high.astype(F32)).astype(BF)
    gap = iota((256, 256), 0) - iota((256, 256), 1)
    one = jnp.ones((256, 256), F32)
    none = jnp.zeros((256, 256), F32)
    band[4] = jnp.where((gap >= NORM_HALF) & (gap <= 3 * NORM_HALF), one, none).astype(BF)
    band[5] = jnp.where((gap <= -NORM_HALF) & (gap >= -3 * NORM_HALF), one, none).astype(BF)
    band[6] = jnp.where(iota((256, 256), 0) + iota((256, 256), 1) == 255, one, none).astype(BF)

    own = (z * NY + y) * NC + core
    lanes = iota((128, 128), 1)
    subs = iota((128, 128), 0)
    row = jnp.full((8, 128), -1, jnp.int32)
    for s in range(S):
        row = jnp.where(lane == s, index[s], row)
    rows = jnp.concatenate([row] * 16, axis=0)
    inside = (rows >= own * CHN) & (rows < own * CHN + CHN)
    fone, fnone = jnp.ones((128, 128), F32), jnp.zeros((128, 128), F32)
    mine = jnp.where(inside, fone, fnone)
    before = jnp.where(subs < lanes, fone, fnone)
    rank = dot(mine.astype(BF), before.astype(BF))
    hit = jnp.where(inside & (rows == own * CHN + subs), fone, fnone).astype(BF)[0:CHN]
    subf = subs.astype(F32)
    for i in range(4):
        slot = jnp.where(inside & (subf == rank + SLOTS * i), fone, fnone).astype(BF)[0:48]
        pick[i] = dot_t(slot, hit).astype(BF)

    colsum = jnp.sum(jnp.where(subs == lanes, rows.astype(F32), fnone), axis=1, keepdims=True)
    owner_col = jnp.floor((colsum + 0.5) * (1.0 / CHN))
    owner_row = jnp.floor((rows.astype(F32) + 0.5) * (1.0 / CHN))
    rank_col = jnp.sum(
        jnp.where((owner_row == owner_col) & (lanes < subs), fone, fnone), axis=1, keepdims=True
    )
    residue = owner_col - 8.0 * jnp.floor(owner_col * 0.125)
    place = (residue * ROWS + rank_col)[0:S]
    wide = iota((S, 8 * ROWS), 1).astype(F32)
    uone, unone = jnp.ones((S, 8 * ROWS), F32), jnp.zeros((S, 8 * ROWS), F32)
    for e in range(NP + 2):
        offset = 96 if e == 0 else 112 if e == NP + 1 else SLOTS * ORDER.index(e - 1)
        unp[e * S:(e + 1) * S, :] = jnp.where(wide == place + offset, uone, unone).astype(BF)

    def put(group, half, block):
        high = block.astype(BF)
        at = (slice(group * CHN, group * CHN + CHN), slice(half * 128, half * 128 + 128))
        xh[at] = high
        xl[at] = (block - high.astype(F32)).astype(BF)

    load.wait()
    for b in range(NB):
        put(1 + b // 2, b % 2, xbuf[:, b * 128:b * 128 + 128])
    nothing = jnp.zeros((CHN, 128), F32)
    put(0, 0, nothing)
    put(NP + 1, 1, nothing)

    def filtered(lo, hi):
        n = slice(lo * CHN, hi * CHN)
        m = slice((lo + 1) * CHN, (hi + 1) * CHN)
        value = dot_t(xh[n], band[0]) + dot_t(xh[m], band[2])
        value += dot_t(xl[n], band[0]) + dot_t(xl[m], band[2])
        value += dot_t(xh[n], band[1]) + dot_t(xh[m], band[3])
        return value

    def keep(lo, hi, value):
        n = slice(lo * CHN, hi * CHN)
        fbuf[n] = value
        size = jnp.abs(value)
        high = size.astype(BF)
        fa[n] = high
        fb[n] = (size - high.astype(F32)).astype(BF)

    def normalize(lo, hi):
        first, second = slice(lo * CHN, hi * CHN), slice((lo + 1) * CHN, (hi + 1) * CHN)
        level = dot(fa[first], band[4]) + dot(fa[second], band[5])
        level += dot(fb[first], band[4]) + dot(fb[second], band[5])
        below = EPSILON + level / (2 * NORM_HALF + 1)
        nb[first, 0:128] = (fbuf[first, 128:256] / below[:, 0:128]).astype(BF)
        nb[first, 128:256] = (fbuf[second, 0:128] / below[:, 128:256]).astype(BF)

    def pair(p):
        return nb[p * CHN:(p + 1) * CHN]

    def fold(j):
        total = dot(pick[0], pair(ORDER[4 * j]))
        for i in range(1, 4):
            total += dot(pick[i], pair(ORDER[4 * j + i]))
        pack[48 * j:48 * j + 48, :] = total.astype(BF)

    def part(ref, k):
        at, size = CHUNKS[k]
        return ref.at[at:at + size]

    def ring(d, far, k):
        slots, two, near = (zu, up2_z, up_z) if d == 0 else (zd, dn2_z, dn_z)
        src = part(pack, k) if far < 2 else part(slots.at[1], k)
        peer = (near, two, near, two)[far]
        return remote(src, part(slots.at[far], k), zsem.at[d, far, k], peer)

    def rings(far, k):
        return [d for d in range(2) if far < 3 or (d == 0) == UP[k]]

    started = [to_right, to_left]

    def go(copy):
        copy.start()
        started.append(copy)

    def send(k):
        for far in (1, 0):
            for d in range(2):
                go(ring(d, far, k))

    keep(1, NP, filtered(1, NP))
    normalize(1, NP - 1)
    fold(0)
    send(0)
    to_right.wait_recv()
    to_left.wait_recv()
    put(0, 1, jnp.where(x > 0, halo[0], nothing))
    put(NP + 1, 0, jnp.where(x < NX - 1, halo[1], nothing))
    ends = iota((CHN, 256), 1)
    empty = jnp.zeros((CHN, 256), F32)
    keep(0, 1, jnp.where((ends >= 128) | (x > 0), filtered(0, 1), empty))
    keep(NP, NP + 1, jnp.where((ends < 128) | (x < NX - 1), filtered(NP, NP + 1), empty))
    normalize(0, 1)
    normalize(NP - 1, NP)
    lower = dot(pick[0], pair(0))[0:16]
    upper = dot(pick[0], pair(NP - 1))[0:16]
    edge[0] = jnp.where(x > 0, lower, jnp.zeros_like(lower)).astype(BF)
    edge[1] = jnp.where(x < NX - 1, upper, jnp.zeros_like(upper)).astype(BF)

    edge_left = remote(edge.at[0], pack.at[112:128], esem.at[0], left)
    edge_right = remote(edge.at[1], pack.at[96:112], esem.at[1], right)
    go(edge_left)
    go(edge_right)
    fold(1)
    send(1)
    turned = dot(nb[...], band[6]).astype(BF)
    for p in range(NP):
        nrev[:, (NP - 1 - p) * 256:(NP - p) * 256] = turned[p * CHN:(p + 1) * CHN]
    save = pltpu.make_async_copy(nrev, nr_out, lsem.at[1])
    save.start()

    def onward(k):
        for d in range(2):
            ring(d, 1, k).wait_recv()
            go(ring(d, 2, k))
            if d in rings(3, k):
                go(ring(d, 3, k))

    onward(0)
    edge_left.wait_recv()
    edge_right.wait_recv()
    send(2)
    onward(1)
    onward(2)

    me = y * NC + core

    def hold(slot, k):
        at, size = CHUNKS[k]
        return gath.at[slot, at:at + size]

    low, high = lax.rem(y + NY - 1, NY) * NC + core, lax.rem(y + 1, NY) * NC + core
    far = lax.rem(y + 2, NY) * NC + core
    origin = (me, low, high, far)

    def line(kind, k):
        return remote(hold(me, k), hold(me, k), ysem.at[kind, k], (up_y, dn_y, far_y)[kind])

    def across(n, k):
        return remote(hold(origin[n], k), hold(origin[n], k), csem.at[n, k], other)

    for k in range(3):
        at, size = CHUNKS[k]
        total = pack[at:at + size]
        for far in (0, 2, 3):
            for d in rings(far, k):
                ring(d, far, k).wait_recv()
        for far in range(3):
            total += zu[far, at:at + size] + zd[far, at:at + size]
        total += (zu if UP[k] else zd)[3, at:at + size]
        gath[me, at:at + size] = total
        for kind in (2, 0, 1):
            go(line(kind, k))
        go(across(0, k))
    for k in range(3):
        for kind in range(3):
            line(kind, k).wait_recv()
            go(across(1 + kind, k))
    for n in range(4):
        for k in range(3):
            across(n, k).wait_recv()

    spread = dot(unp[...], gath[...].reshape(8 * ROWS, 256))
    for e in range(NP + 2):
        for h in range(2):
            src_out[2 * e + h] = spread[e * S:(e + 1) * S, h * 128:h * 128 + 128]
    for copy in started:
        copy.wait_send()
    save.wait()


def gather(traces, fir, index):
    dma = pltpu.SemaphoreType.DMA
    return pl.pallas_call(
        gather_kernel,
        in_specs=[
            pl.BlockSpec(memory_space=pl.ANY),
            pl.BlockSpec(memory_space=pltpu.SMEM),
            pl.BlockSpec(memory_space=pltpu.SMEM),
        ],
        out_specs=[pl.BlockSpec(memory_space=pltpu.VMEM), pl.BlockSpec(memory_space=pl.ANY)],
        out_shape=[
            jax.ShapeDtypeStruct((NB + 4, S, 128), F32),
            jax.ShapeDtypeStruct((CHN, T), BF),
        ],
        scratch_shapes=[
            pltpu.VMEM((CHN, T), F32),
            pltpu.VMEM((2, CHN, 128), F32),
            pltpu.VMEM(((NP + 2) * CHN, 256), BF),
            pltpu.VMEM(((NP + 2) * CHN, 256), BF),
            pltpu.VMEM((7, 256, 256), BF),
            pltpu.VMEM(((NP + 1) * CHN, 256), F32),
            pltpu.VMEM(((NP + 1) * CHN, 256), BF),
            pltpu.VMEM(((NP + 1) * CHN, 256), BF),
            pltpu.VMEM((NP * CHN, 256), BF),
            pltpu.VMEM((CHN, T), BF),
            pltpu.VMEM((4, 48, CHN), BF),
            pltpu.VMEM((2, 16, 256), BF),
            pltpu.VMEM((ROWS, 256), BF),
            pltpu.VMEM((4, ROWS, 256), BF),
            pltpu.VMEM((4, ROWS, 256), BF),
            pltpu.VMEM((8, ROWS, 256), BF),
            pltpu.VMEM(((NP + 2) * S, 8 * ROWS), BF),
            dma((2,)),
            dma((2, 2)),
            dma((2, 2)),
            dma((2, 4, 3, 2)),
            dma((3, 3, 2)),
            dma((4, 3, 2)),
        ],
        compiler_params=pltpu.CompilerParams(
            collective_id=0, has_side_effects=True, vmem_limit_bytes=63 << 20
        ),
        name="gather",
    )(traces, fir, index)


def corr_kernel(src_ref, nr_ref, o_ref, w_ref, h0, h1):
    g = pl.program_id(0)
    keep = iota((128, 128), 1) > iota((128, 128), 0)

    def build(h, s, half):
        cols = slice(half * 128, half * 128 + 128)

        def turn(b):
            x = src_ref.at[b][pl.ds(s, 128, stride=0), :]
            return pltpu.roll(x, 1, 1, stride=1, stride_axis=0)

        prev = turn(KB)
        for q in range(KB):
            cur = turn(KB - 1 - q)
            h[q * 128:(q + 1) * 128, cols] = jnp.where(keep, prev, cur).astype(BF)
            prev = cur

    @pl.when(g == 0)
    def _():
        w_ref[...] = jnp.zeros_like(w_ref)
        for a in range(4):
            w_ref[a * CHN:(a + 1) * CHN, (3 - a) * 128:(3 - a) * 128 + T] = nr_ref[...]
        for i in range(WIDE):
            build(h0, i, i)

    bufs = (h0, h1)
    for p in range(STEP // WIDE):
        nxt = lax.rem(g * STEP + WIDE * (p + 1), S)
        for i in range(WIDE):
            build(bufs[(p + 1) % 2], nxt + i, i)
        h = bufs[p % 2]
        res = dot(w_ref[:, 256:2048], h[256:2048, :])
        low = dot(w_ref[2 * CHN:, 0:256], h[0:256, :])
        high = dot(w_ref[:3 * CHN, 2048:2304], h[2048:2304, :])
        last = dot(w_ref[:CHN, 2304:], h[2304:, :])
        parts = [res[a * CHN:(a + 1) * CHN] for a in range(4)]
        for a in (2, 3):
            parts[a] += low[(a - 2) * CHN:(a - 1) * CHN]
        for a in (0, 1, 2):
            parts[a] += high[a * CHN:(a + 1) * CHN]
        parts[0] += last
        for a in range(4):
            for i in range(WIDE):
                o_ref[WIDE * p + i, :, a * 128:(a + 1) * 128] = parts[a][
                    :, i * 128:(i + 1) * 128
                ] * (1.0 / math.sqrt(T))


def corr(src_ext, nr):
    return pl.pallas_call(
        corr_kernel,
        grid=(S // STEP,),
        in_specs=[
            pl.BlockSpec((KB + 1, S, 128), lambda g: (0, 0, 0)),
            pl.BlockSpec((CHN, T), lambda g: (0, 0)),
        ],
        out_specs=pl.BlockSpec((STEP, CHN, 2 * LAG_HALF), lambda g: (g, 0, 0)),
        out_shape=jax.ShapeDtypeStruct((S, CHN, 2 * LAG_HALF), F32),
        scratch_shapes=[
            pltpu.VMEM((4 * CHN, K), BF),
            pltpu.VMEM((K, WIDE * 128), BF),
            pltpu.VMEM((K, WIDE * 128), BF),
        ],
        compiler_params=pltpu.CompilerParams(
            dimension_semantics=("arbitrary",), vmem_limit_bytes=63 << 20
        ),
        name="corr",
    )(src_ext, nr)


def body(traces, fir_taps, source_index):
    src_ext, nr = gather(traces, fir_taps, source_index)
    return corr(src_ext, nr)[None]


def solution(mesh):
    torus = Mesh(mesh.devices.reshape(NZ, NY, NC, NX), AXES)
    chan = AXES[:3]
    return jax.shard_map(
        body,
        mesh=torus,
        in_specs=(P(chan, "tm"), P(), P()),
        out_specs=P("tm", None, chan, None),
        check_vma=False,
    )
```

```python
import math

import jax
import jax.numpy as jnp
from jax import lax
from jax.experimental import pallas as pl
from jax.experimental.pallas import tpu as pltpu
from jax.sharding import Mesh
from jax.sharding import PartitionSpec as P

CHN, T, S = 80, 2048, 64
EPSILON = 1e-05
FIR_HALF, NORM_HALF, LAG_HALF = 32, 64, 256
TAPS = 2 * FIR_HALF + 1
SLOTS = 12
NB = T // 128
NP = T // 256
KB = NB + 3
K = KB * 128
STEP = 16
WIDE = 4
VA, VB = 16, 24
AXES = ("chan_0", "chan_1", "chan_2", "tm")
NZ, NY, NC, NX = 8, 4, 2, 4
CHUNKS = ((0, 48), (48, 48), (96, 32))
UP = (True, False, True)
ROWS = 128
ORDER = (1, 2, 3, 4, 5, 6, 0, 7)
BF = jnp.bfloat16
F32 = jnp.float32


def dot(a, b):
    return jnp.dot(a, b, preferred_element_type=F32)


def dot_t(a, b):
    return lax.dot_general(a, b, (((1,), (1,)), ((), ())), preferred_element_type=F32)


def iota(shape, dim):
    return lax.broadcasted_iota(jnp.int32, shape, dim)


def gather_kernel(
    traces, fir_in, index_in, src_out, nr_out,
    fir, index, xbuf, halo, xh, xl, band, fbuf, fa, fb, nb, pick, edge, pack, zu, zd, gath, unp,
    lsem, hsem, esem, zsem, ysem, csem,
):
    z, y, core, x = (lax.axis_index(a) for a in AXES)
    up_z = {"chan_0": lax.rem(z + 1, NZ)}
    dn_z = {"chan_0": lax.rem(z + NZ - 1, NZ)}
    up2_z = {"chan_0": lax.rem(z + 2, NZ)}
    dn2_z = {"chan_0": lax.rem(z + NZ - 2, NZ)}
    up_y = {"chan_1": lax.rem(y + 1, NY)}
    dn_y = {"chan_1": lax.rem(y + NY - 1, NY)}
    far_y = {"chan_1": lax.rem(y + 2, NY)}
    other = {"chan_2": 1 - core}
    right = {"tm": lax.rem(x + 1, NX)}
    left = {"tm": lax.rem(x + NX - 1, NX)}

    load = pltpu.make_async_copy(traces, xbuf, lsem.at[0])
    load.start()
    taps_load = pltpu.make_async_copy(fir_in, fir, lsem.at[1])
    taps_load.start()
    index_load = pltpu.make_async_copy(index_in, index, lsem.at[2])
    index_load.start()
    barrier = pltpu.get_barrier_semaphore()
    peers = (up2_z, dn2_z, up_z, dn_z, far_y, up_y, dn_y, other, right, left)
    for peer in peers:
        pl.semaphore_signal(barrier, inc=1, device_id=peer, device_id_type=pl.DeviceIdType.MESH)
    pl.semaphore_wait(barrier, len(peers))

    def remote(src, dst, sems, peer):
        return pltpu.make_async_remote_copy(
            src_ref=src, dst_ref=dst, send_sem=sems.at[0], recv_sem=sems.at[1],
            device_id=peer, device_id_type=pl.DeviceIdType.MESH,
        )

    to_right = remote(traces.at[:, T - 128:T], halo.at[0], hsem.at[0], right)
    to_left = remote(traces.at[:, 0:128], halo.at[1], hsem.at[1], left)
    to_right.start()
    to_left.start()

    taps_load.wait()
    index_load.wait()
    lane = iota((8, 128), 1)
    taps = jnp.zeros((8, 128), F32)
    for k in range(TAPS):
        taps = jnp.where(lane == k, fir[k], taps)
    rolled = pltpu.roll(jnp.concatenate([taps] * 16, axis=0), 128 - FIR_HALF, 1, stride=1, stride_axis=0)
    apart = iota((128, 128), 1) - iota((128, 128), 0)
    zero = jnp.zeros((128, 128), F32)
    d1 = jnp.where(apart >= 128 - FIR_HALF, rolled, zero)
    d2 = jnp.where(jnp.abs(apart) <= FIR_HALF, rolled, zero)
    d3 = jnp.where(apart <= FIR_HALF - 128, rolled, zero)
    for n, blocks in enumerate((((d1, d2), (zero, d1)), ((d3, zero), (d2, d3)))):
        for i in range(2):
            for u in range(2):
                whole = blocks[i][u]
                high = whole.astype(BF)
                at = (slice(i * 128, i * 128 + 128), slice(u * 128, u * 128 + 128))
                band[(2 * n,) + at] = high
                band[(2 * n + 1,) + at] = (whole - high.astype(F32)).astype(BF)
    gap = iota((256, 256), 0) - iota((256, 256), 1)
    one = jnp.ones((256, 256), F32)
    none = jnp.zeros((256, 256), F32)
    band[4] = jnp.where((gap >= NORM_HALF) & (gap <= 3 * NORM_HALF), one, none).astype(BF)
    band[5] = jnp.where((gap <= -NORM_HALF) & (gap >= -3 * NORM_HALF), one, none).astype(BF)
    band[6] = jnp.where(iota((256, 256), 0) + iota((256, 256), 1) == 255, one, none).astype(BF)

    own = (z * NY + y) * NC + core
    lanes = iota((128, 128), 1)
    subs = iota((128, 128), 0)
    row = jnp.full((8, 128), -1, jnp.int32)
    for s in range(S):
        row = jnp.where(lane == s, index[s], row)
    rows = jnp.concatenate([row] * 16, axis=0)
    inside = (rows >= own * CHN) & (rows < own * CHN + CHN)
    fone, fnone = jnp.ones((128, 128), F32), jnp.zeros((128, 128), F32)
    mine = jnp.where(inside, fone, fnone)
    before = jnp.where(subs < lanes, fone, fnone)
    rank = dot(mine.astype(BF), before.astype(BF))
    hit = jnp.where(inside & (rows == own * CHN + subs), fone, fnone).astype(BF)[0:CHN]
    subf = subs.astype(F32)
    for i in range(4):
        slot = jnp.where(inside & (subf == rank + SLOTS * i), fone, fnone).astype(BF)[0:48]
        pick[i] = dot_t(slot, hit).astype(BF)

    colsum = jnp.sum(jnp.where(subs == lanes, rows.astype(F32), fnone), axis=1, keepdims=True)
    owner_col = jnp.floor((colsum + 0.5) * (1.0 / CHN))
    owner_row = jnp.floor((rows.astype(F32) + 0.5) * (1.0 / CHN))
    rank_col = jnp.sum(
        jnp.where((owner_row == owner_col) & (lanes < subs), fone, fnone), axis=1, keepdims=True
    )
    residue = owner_col - 8.0 * jnp.floor(owner_col * 0.125)
    place = (residue * ROWS + rank_col)[0:S]
    wide = iota((S, 8 * ROWS), 1).astype(F32)
    uone, unone = jnp.ones((S, 8 * ROWS), F32), jnp.zeros((S, 8 * ROWS), F32)
    for e in range(NP + 2):
        offset = 96 if e == 0 else 112 if e == NP + 1 else SLOTS * ORDER.index(e - 1)
        unp[e * S:(e + 1) * S, :] = jnp.where(wide == place + offset, uone, unone).astype(BF)

    def put(group, half, block):
        high = block.astype(BF)
        at = (slice(group * CHN, group * CHN + CHN), slice(half * 128, half * 128 + 128))
        xh[at] = high
        xl[at] = (block - high.astype(F32)).astype(BF)

    load.wait()
    for b in range(NB):
        put(1 + b // 2, b % 2, xbuf[:, b * 128:b * 128 + 128])
    nothing = jnp.zeros((CHN, 128), F32)
    put(0, 0, nothing)
    put(NP + 1, 1, nothing)

    def filtered(lo, hi):
        n = slice(lo * CHN, hi * CHN)
        m = slice((lo + 1) * CHN, (hi + 1) * CHN)
        value = dot_t(xh[n], band[0]) + dot_t(xh[m], band[2])
        value += dot_t(xl[n], band[0]) + dot_t(xl[m], band[2])
        value += dot_t(xh[n], band[1]) + dot_t(xh[m], band[3])
        return value

    def keep(lo, hi, value):
        n = slice(lo * CHN, hi * CHN)
        fbuf[n] = value
        size = jnp.abs(value)
        high = size.astype(BF)
        fa[n] = high
        fb[n] = (size - high.astype(F32)).astype(BF)

    def normalize(lo, hi):
        first, second = slice(lo * CHN, hi * CHN), slice((lo + 1) * CHN, (hi + 1) * CHN)
        level = dot(fa[first], band[4]) + dot(fa[second], band[5])
        level += dot(fb[first], band[4]) + dot(fb[second], band[5])
        below = EPSILON + level / (2 * NORM_HALF + 1)
        nb[first, 0:128] = (fbuf[first, 128:256] / below[:, 0:128]).astype(BF)
        nb[first, 128:256] = (fbuf[second, 0:128] / below[:, 128:256]).astype(BF)

    def pair(p):
        return nb[p * CHN:(p + 1) * CHN]

    def fold(j):
        total = dot(pick[0], pair(ORDER[4 * j]))
        for i in range(1, 4):
            total += dot(pick[i], pair(ORDER[4 * j + i]))
        pack[48 * j:48 * j + 48, :] = total.astype(BF)

    def part(ref, k):
        at, size = CHUNKS[k]
        return ref.at[at:at + size]

    def ring(d, far, k):
        slots, two, near = (zu, up2_z, up_z) if d == 0 else (zd, dn2_z, dn_z)
        src = part(pack, k) if far < 2 else part(slots.at[1], k)
        peer = (near, two, near, two)[far]
        return remote(src, part(slots.at[far], k), zsem.at[d, far, k], peer)

    def rings(far, k):
        return [d for d in range(2) if far < 3 or (d == 0) == UP[k]]

    started = [to_right, to_left]

    def go(copy):
        copy.start()
        started.append(copy)

    def send(k):
        for far in (1, 0):
            for d in range(2):
                go(ring(d, far, k))

    keep(1, NP, filtered(1, NP))
    normalize(1, NP - 1)
    fold(0)
    send(0)
    to_right.wait_recv()
    to_left.wait_recv()
    put(0, 1, jnp.where(x > 0, halo[0], nothing))
    put(NP + 1, 0, jnp.where(x < NX - 1, halo[1], nothing))
    ends = iota((CHN, 256), 1)
    empty = jnp.zeros((CHN, 256), F32)
    keep(0, 1, jnp.where((ends >= 128) | (x > 0), filtered(0, 1), empty))
    keep(NP, NP + 1, jnp.where((ends < 128) | (x < NX - 1), filtered(NP, NP + 1), empty))
    normalize(0, 1)
    normalize(NP - 1, NP)
    lower = dot(pick[0], pair(0))[0:16]
    upper = dot(pick[0], pair(NP - 1))[0:16]
    edge[0] = jnp.where(x > 0, lower, jnp.zeros_like(lower)).astype(BF)
    edge[1] = jnp.where(x < NX - 1, upper, jnp.zeros_like(upper)).astype(BF)

    edge_left = remote(edge.at[0], pack.at[112:128], esem.at[0], left)
    edge_right = remote(edge.at[1], pack.at[96:112], esem.at[1], right)
    go(edge_left)
    go(edge_right)
    fold(1)
    send(1)
    turned = dot(nb[...], band[6]).astype(BF)
    for p in range(NP):
        nr_out[:, (NP - 1 - p) * 256:(NP - p) * 256] = turned[p * CHN:(p + 1) * CHN]

    def onward(k):
        for d in range(2):
            ring(d, 1, k).wait_recv()
            go(ring(d, 2, k))
            if d in rings(3, k):
                go(ring(d, 3, k))

    onward(0)
    edge_left.wait_recv()
    edge_right.wait_recv()
    send(2)
    onward(1)
    onward(2)

    me = y * NC + core

    def hold(slot, k):
        at, size = CHUNKS[k]
        return gath.at[slot, at:at + size]

    low, high = lax.rem(y + NY - 1, NY) * NC + core, lax.rem(y + 1, NY) * NC + core
    far = lax.rem(y + 2, NY) * NC + core
    origin = (me, low, high, far)

    def line(kind, k):
        return remote(hold(me, k), hold(me, k), ysem.at[kind, k], (up_y, dn_y, far_y)[kind])

    def across(n, k):
        return remote(hold(origin[n], k), hold(origin[n], k), csem.at[n, k], other)

    for k in range(3):
        at, size = CHUNKS[k]
        total = pack[at:at + size]
        for far in (0, 2, 3):
            for d in rings(far, k):
                ring(d, far, k).wait_recv()
        for far in range(3):
            total += zu[far, at:at + size] + zd[far, at:at + size]
        total += (zu if UP[k] else zd)[3, at:at + size]
        gath[me, at:at + size] = total
        for kind in (2, 0, 1):
            go(line(kind, k))
        go(across(0, k))
    for k in range(3):
        for kind in range(3):
            line(kind, k).wait_recv()
            go(across(1 + kind, k))
    for n in range(4):
        for k in range(3):
            across(n, k).wait_recv()

    spread = dot(unp[...], gath[...].reshape(8 * ROWS, 256))
    for e in range(NP + 2):
        for h in range(2):
            src_out[2 * e + h] = spread[e * S:(e + 1) * S, h * 128:h * 128 + 128]
    for copy in started:
        copy.wait_send()


def gather(traces, fir, index):
    dma = pltpu.SemaphoreType.DMA
    return pl.pallas_call(
        gather_kernel,
        in_specs=[
            pl.BlockSpec(memory_space=pltpu.HBM),
            pl.BlockSpec(memory_space=pltpu.HBM),
            pl.BlockSpec(memory_space=pltpu.HBM),
        ],
        out_specs=[pl.BlockSpec(memory_space=pltpu.VMEM)] * 2,
        out_shape=[
            jax.ShapeDtypeStruct((NB + 4, S, 128), F32),
            jax.ShapeDtypeStruct((CHN, T), BF),
        ],
        scratch_shapes=[
            pltpu.SMEM((TAPS,), F32),
            pltpu.SMEM((S,), jnp.int32),
            pltpu.VMEM((CHN, T), F32),
            pltpu.VMEM((2, CHN, 128), F32),
            pltpu.VMEM(((NP + 2) * CHN, 256), BF),
            pltpu.VMEM(((NP + 2) * CHN, 256), BF),
            pltpu.VMEM((7, 256, 256), BF),
            pltpu.VMEM(((NP + 1) * CHN, 256), F32),
            pltpu.VMEM(((NP + 1) * CHN, 256), BF),
            pltpu.VMEM(((NP + 1) * CHN, 256), BF),
            pltpu.VMEM((NP * CHN, 256), BF),
            pltpu.VMEM((4, 48, CHN), BF),
            pltpu.VMEM((2, 16, 256), BF),
            pltpu.VMEM((ROWS, 256), BF),
            pltpu.VMEM((4, ROWS, 256), BF),
            pltpu.VMEM((4, ROWS, 256), BF),
            pltpu.VMEM((8, ROWS, 256), BF),
            pltpu.VMEM(((NP + 2) * S, 8 * ROWS), BF),
            dma((3,)),
            dma((2, 2)),
            dma((2, 2)),
            dma((2, 4, 3, 2)),
            dma((3, 3, 2)),
            dma((4, 3, 2)),
        ],
        compiler_params=pltpu.CompilerParams(
            collective_id=0, has_side_effects=True, vmem_limit_bytes=VA << 20
        ),
        name="gather",
    )(*(pltpu.with_memory_space_constraint(v, pltpu.HBM) for v in (traces, fir, index)))


def corr_kernel(src_ref, nr_ref, o_ref, w_ref, h0, h1):
    g = pl.program_id(0)
    keep = iota((128, 128), 1) > iota((128, 128), 0)

    def build(h, s, half):
        cols = slice(half * 128, half * 128 + 128)

        def turn(b):
            x = src_ref.at[b][pl.ds(s, 128, stride=0), :]
            return pltpu.roll(x, 1, 1, stride=1, stride_axis=0)

        prev = turn(KB)
        for q in range(KB):
            cur = turn(KB - 1 - q)
            h[q * 128:(q + 1) * 128, cols] = jnp.where(keep, prev, cur).astype(BF)
            prev = cur

    @pl.when(g == 0)
    def _():
        w_ref[...] = jnp.zeros_like(w_ref)
        for a in range(4):
            w_ref[a * CHN:(a + 1) * CHN, (3 - a) * 128:(3 - a) * 128 + T] = nr_ref[...]
        for i in range(WIDE):
            build(h0, i, i)

    bufs = (h0, h1)
    for p in range(STEP // WIDE):
        nxt = lax.rem(g * STEP + WIDE * (p + 1), S)
        for i in range(WIDE):
            build(bufs[(p + 1) % 2], nxt + i, i)
        h = bufs[p % 2]
        res = dot(w_ref[:, 256:2048], h[256:2048, :])
        low = dot(w_ref[2 * CHN:, 0:256], h[0:256, :])
        high = dot(w_ref[:3 * CHN, 2048:2304], h[2048:2304, :])
        last = dot(w_ref[:CHN, 2304:], h[2304:, :])
        parts = [res[a * CHN:(a + 1) * CHN] for a in range(4)]
        for a in (2, 3):
            parts[a] += low[(a - 2) * CHN:(a - 1) * CHN]
        for a in (0, 1, 2):
            parts[a] += high[a * CHN:(a + 1) * CHN]
        parts[0] += last
        for a in range(4):
            for i in range(WIDE):
                o_ref[WIDE * p + i, :, a * 128:(a + 1) * 128] = parts[a][
                    :, i * 128:(i + 1) * 128
                ] * (1.0 / math.sqrt(T))


def corr(src_ext, nr):
    return pl.pallas_call(
        corr_kernel,
        grid=(S // STEP,),
        in_specs=[
            pl.BlockSpec(memory_space=pltpu.VMEM),
            pl.BlockSpec(memory_space=pltpu.VMEM),
        ],
        out_specs=pl.BlockSpec((STEP, CHN, 2 * LAG_HALF), lambda g: (g, 0, 0)),
        out_shape=jax.ShapeDtypeStruct((S, CHN, 2 * LAG_HALF), F32),
        scratch_shapes=[
            pltpu.VMEM((4 * CHN, K), BF),
            pltpu.VMEM((K, WIDE * 128), BF),
            pltpu.VMEM((K, WIDE * 128), BF),
        ],
        compiler_params=pltpu.CompilerParams(
            dimension_semantics=("arbitrary",), vmem_limit_bytes=VB << 20
        ),
        name="corr",
    )(src_ext, nr)


def body(traces, fir_taps, source_index):
    src_ext, nr = gather(traces, fir_taps, source_index)
    return corr(src_ext, nr)[None]


def solution(mesh):
    torus = Mesh(mesh.devices.reshape(NZ, NY, NC, NX), AXES)
    chan = AXES[:3]
    return jax.shard_map(
        body,
        mesh=torus,
        in_specs=(P(chan, "tm"), P(), P()),
        out_specs=P("tm", None, chan, None),
        check_vma=False,
    )
```

```python
import math

import jax
import jax.numpy as jnp
from jax import lax
from jax.experimental import pallas as pl
from jax.experimental.pallas import tpu as pltpu
from jax.sharding import Mesh
from jax.sharding import PartitionSpec as P

CHN, T, S = 80, 2048, 64
EPSILON = 1e-05
FIR_HALF, NORM_HALF, LAG_HALF = 32, 64, 256
TAPS = 2 * FIR_HALF + 1
SLOTS = 12
NB = T // 128
NP = T // 256
KB = NB + 3
K = KB * 128
STEP = 16
WIDE = 4
VA, VB = 16, 24
AXES = ("chan_0", "chan_1", "chan_2", "tm")
NZ, NY, NC, NX = 8, 4, 2, 4
CHUNKS = ((0, 48), (48, 48), (96, 32))
UP = (True, False, True)
ROWS = 128
ORDER = (1, 2, 3, 4, 5, 6, 0, 7)
BF = jnp.bfloat16
F32 = jnp.float32


def dot(a, b):
    return jnp.dot(a, b, preferred_element_type=F32)


def dot_t(a, b):
    return lax.dot_general(a, b, (((1,), (1,)), ((), ())), preferred_element_type=F32)


def iota(shape, dim):
    return lax.broadcasted_iota(jnp.int32, shape, dim)


def gather_kernel(
    traces, fir_in, index_in, src_out, nr_out,
    fir, index, xbuf, halo, xh, xl, band, fbuf, fa, fb, nb, pick, edge, pack, zu, zd, gath, unp,
    lsem, hsem, esem, zsem, ysem, csem,
):
    z, y, core, x = (lax.axis_index(a) for a in AXES)
    up_z = {"chan_0": lax.rem(z + 1, NZ)}
    dn_z = {"chan_0": lax.rem(z + NZ - 1, NZ)}
    up2_z = {"chan_0": lax.rem(z + 2, NZ)}
    dn2_z = {"chan_0": lax.rem(z + NZ - 2, NZ)}
    up_y = {"chan_1": lax.rem(y + 1, NY)}
    dn_y = {"chan_1": lax.rem(y + NY - 1, NY)}
    far_y = {"chan_1": lax.rem(y + 2, NY)}
    other = {"chan_2": 1 - core}
    right = {"tm": lax.rem(x + 1, NX)}
    left = {"tm": lax.rem(x + NX - 1, NX)}

    load = pltpu.make_async_copy(traces, xbuf, lsem.at[0])
    load.start()
    taps_load = pltpu.make_async_copy(fir_in, fir, lsem.at[1])
    taps_load.start()
    index_load = pltpu.make_async_copy(index_in, index, lsem.at[2])
    index_load.start()
    barrier = pltpu.get_barrier_semaphore()
    peers = (up2_z, dn2_z, up_z, dn_z, far_y, up_y, dn_y, other, right, left)
    for peer in peers:
        pl.semaphore_signal(barrier, inc=1, device_id=peer, device_id_type=pl.DeviceIdType.MESH)
    pl.semaphore_wait(barrier, len(peers))

    def remote(src, dst, sems, peer):
        return pltpu.make_async_remote_copy(
            src_ref=src, dst_ref=dst, send_sem=sems.at[0], recv_sem=sems.at[1],
            device_id=peer, device_id_type=pl.DeviceIdType.MESH,
        )

    to_right = remote(traces.at[:, T - 128:T], halo.at[0], hsem.at[0], right)
    to_left = remote(traces.at[:, 0:128], halo.at[1], hsem.at[1], left)
    to_right.start()
    to_left.start()

    taps_load.wait()
    index_load.wait()
    lane = iota((8, 128), 1)
    taps = jnp.zeros((8, 128), F32)
    for k in range(TAPS):
        taps = jnp.where(lane == k, fir[TAPS - 1 - k], taps)
    rolled = pltpu.roll(jnp.concatenate([taps] * 16, axis=0), 128 - FIR_HALF, 1, stride=1, stride_axis=0)
    apart = iota((128, 128), 1) - iota((128, 128), 0)
    zero = jnp.zeros((128, 128), F32)
    d1 = jnp.where(apart <= FIR_HALF - 128, rolled, zero)
    d2 = jnp.where(jnp.abs(apart) <= FIR_HALF, rolled, zero)
    d3 = jnp.where(apart >= 128 - FIR_HALF, rolled, zero)
    for n, blocks in enumerate((((d1, zero), (d2, d1)), ((d3, d2), (zero, d3)))):
        for u in range(2):
            for i in range(2):
                whole = blocks[u][i]
                high = whole.astype(BF)
                at = (slice(u * 128, u * 128 + 128), slice(i * 128, i * 128 + 128))
                band[(2 * n,) + at] = high
                band[(2 * n + 1,) + at] = (whole - high.astype(F32)).astype(BF)
    gap = iota((256, 256), 0) - iota((256, 256), 1)
    one = jnp.ones((256, 256), F32)
    none = jnp.zeros((256, 256), F32)
    band[4] = jnp.where((gap >= NORM_HALF) & (gap <= 3 * NORM_HALF), one, none).astype(BF)
    band[5] = jnp.where((gap <= -NORM_HALF) & (gap >= -3 * NORM_HALF), one, none).astype(BF)

    def put(group, half, block):
        high = block.astype(BF)
        at = (slice(group * CHN, group * CHN + CHN), slice(half * 128, half * 128 + 128))
        xh[at] = high
        xl[at] = (block - high.astype(F32)).astype(BF)

    load.wait()
    for b in range(NB):
        put(1 + b // 2, b % 2, xbuf[:, b * 128:b * 128 + 128])
    nothing = jnp.zeros((CHN, 128), F32)
    put(0, 0, nothing)
    put(NP + 1, 1, nothing)

    own = (z * NY + y) * NC + core
    lanes = iota((128, 128), 1)
    subs = iota((128, 128), 0)
    row = jnp.full((8, 128), -1, jnp.int32)
    for s in range(S):
        row = jnp.where(lane == s, index[s], row)
    rows = jnp.concatenate([row] * 16, axis=0)
    inside = (rows >= own * CHN) & (rows < own * CHN + CHN)
    fone, fnone = jnp.ones((128, 128), F32), jnp.zeros((128, 128), F32)
    mine = jnp.where(inside, fone, fnone)
    before = jnp.where(subs < lanes, fone, fnone)
    rank = dot(mine.astype(BF), before.astype(BF))
    hit = jnp.where(inside & (rows == own * CHN + subs), fone, fnone).astype(BF)[0:CHN]
    subf = subs.astype(F32)
    for i in range(4):
        slot = jnp.where(inside & (subf == rank + SLOTS * i), fone, fnone).astype(BF)[0:48]
        pick[i] = dot_t(slot, hit).astype(BF)

    def rows_of(ref, groups):
        return jnp.concatenate([ref[lo * CHN:hi * CHN] for lo, hi in groups], axis=0)

    def after(groups):
        return [(lo + 1, hi + 1) for lo, hi in groups]

    def filtered(groups):
        high = [rows_of(xh, groups), rows_of(xh, after(groups))]
        low = [rows_of(xl, groups), rows_of(xl, after(groups))]
        taken = jnp.concatenate(high + low + high, axis=1)
        return dot(taken, jnp.concatenate([band[n] for n in (0, 2, 0, 2, 1, 3)], axis=0))

    def keep(lo, hi, value):
        n = slice(lo * CHN, hi * CHN)
        fbuf[n] = value
        size = jnp.abs(value)
        high = size.astype(BF)
        fa[n] = high
        fb[n] = (size - high.astype(F32)).astype(BF)

    def normalize(groups):
        taken = [rows_of(ref, part) for ref in (fa, fb) for part in (groups, after(groups))]
        level = dot(
            jnp.concatenate(taken, axis=1),
            jnp.concatenate([band[n] for n in (4, 5, 4, 5)], axis=0),
        )
        below = EPSILON + level / (2 * NORM_HALF + 1)
        at = 0
        for lo, hi in groups:
            size = (hi - lo) * CHN
            first, second = slice(lo * CHN, hi * CHN), slice((lo + 1) * CHN, (hi + 1) * CHN)
            nb[first, 0:128] = (fbuf[first, 128:256] / below[at:at + size, 0:128]).astype(BF)
            nb[first, 128:256] = (fbuf[second, 0:128] / below[at:at + size, 128:256]).astype(BF)
            at += size

    def pair(p):
        return nb[p * CHN:(p + 1) * CHN]

    def fold(j):
        total = dot(pick[0], pair(ORDER[4 * j]))
        for i in range(1, 4):
            total += dot(pick[i], pair(ORDER[4 * j + i]))
        pack[48 * j:48 * j + 48, :] = total.astype(BF)

    def part(ref, k):
        at, size = CHUNKS[k]
        return ref.at[at:at + size]

    def ring(d, far, k):
        slots, two, near = (zu, up2_z, up_z) if d == 0 else (zd, dn2_z, dn_z)
        src = part(pack, k) if far < 2 else part(slots.at[1], k)
        peer = (near, two, near, two)[far]
        return remote(src, part(slots.at[far], k), zsem.at[d, far, k], peer)

    def rings(far, k):
        return [d for d in range(2) if far < 3 or (d == 0) == UP[k]]

    started = [to_right, to_left]

    def go(copy):
        copy.start()
        started.append(copy)

    def send(k):
        for far in (1, 0):
            for d in range(2):
                go(ring(d, far, k))

    keep(1, NP, filtered([(1, NP)]))
    normalize([(1, NP - 1)])
    fold(0)
    send(0)
    to_right.wait_recv()
    to_left.wait_recv()
    put(0, 1, jnp.where(x > 0, halo[0], nothing))
    put(NP + 1, 0, jnp.where(x < NX - 1, halo[1], nothing))
    ends = iota((CHN, 256), 1)
    empty = jnp.zeros((CHN, 256), F32)
    both = filtered([(0, 1), (NP, NP + 1)])
    keep(0, 1, jnp.where((ends >= 128) | (x > 0), both[0:CHN], empty))
    keep(NP, NP + 1, jnp.where((ends < 128) | (x < NX - 1), both[CHN:], empty))
    normalize([(0, 1), (NP - 1, NP)])
    lower = dot(pick[0], pair(0))[0:16]
    upper = dot(pick[0], pair(NP - 1))[0:16]
    edge[0] = jnp.where(x > 0, lower, jnp.zeros_like(lower)).astype(BF)
    edge[1] = jnp.where(x < NX - 1, upper, jnp.zeros_like(upper)).astype(BF)

    edge_left = remote(edge.at[0], pack.at[112:128], esem.at[0], left)
    edge_right = remote(edge.at[1], pack.at[96:112], esem.at[1], right)
    go(edge_left)
    go(edge_right)
    fold(1)
    send(1)
    colsum = jnp.sum(jnp.where(subs == lanes, rows.astype(F32), fnone), axis=1, keepdims=True)
    owner_col = jnp.floor((colsum + 0.5) * (1.0 / CHN))
    owner_row = jnp.floor((rows.astype(F32) + 0.5) * (1.0 / CHN))
    rank_col = jnp.sum(
        jnp.where((owner_row == owner_col) & (lanes < subs), fone, fnone), axis=1, keepdims=True
    )
    residue = owner_col - 8.0 * jnp.floor(owner_col * 0.125)
    place = (residue * ROWS + rank_col)[0:S]
    wide = iota((S, 8 * ROWS), 1).astype(F32)
    uone, unone = jnp.ones((S, 8 * ROWS), F32), jnp.zeros((S, 8 * ROWS), F32)
    for e in range(NP + 2):
        offset = 96 if e == 0 else 112 if e == NP + 1 else SLOTS * ORDER.index(e - 1)
        unp[e * S:(e + 1) * S, :] = jnp.where(wide == place + offset, uone, unone).astype(BF)

    band[6] = jnp.where(iota((256, 256), 0) + iota((256, 256), 1) == 255, one, none).astype(BF)
    turned = dot(nb[...], band[6]).astype(BF)
    for p in range(NP):
        nr_out[:, (NP - 1 - p) * 256:(NP - p) * 256] = turned[p * CHN:(p + 1) * CHN]

    def onward(k):
        for d in range(2):
            ring(d, 1, k).wait_recv()
            go(ring(d, 2, k))
            if d in rings(3, k):
                go(ring(d, 3, k))

    onward(0)
    edge_left.wait_recv()
    edge_right.wait_recv()
    send(2)
    onward(1)
    onward(2)

    me = y * NC + core

    def hold(slot, k):
        at, size = CHUNKS[k]
        return gath.at[slot, at:at + size]

    low, high = lax.rem(y + NY - 1, NY) * NC + core, lax.rem(y + 1, NY) * NC + core
    far = lax.rem(y + 2, NY) * NC + core
    origin = (me, low, high, far)

    def line(kind, k):
        return remote(hold(me, k), hold(me, k), ysem.at[kind, k], (up_y, dn_y, far_y)[kind])

    def across(n, k):
        return remote(hold(origin[n], k), hold(origin[n], k), csem.at[n, k], other)

    for k in range(3):
        at, size = CHUNKS[k]
        total = pack[at:at + size]
        for far in (0, 2, 3):
            for d in rings(far, k):
                ring(d, far, k).wait_recv()
        for far in range(3):
            total += zu[far, at:at + size] + zd[far, at:at + size]
        total += (zu if UP[k] else zd)[3, at:at + size]
        gath[me, at:at + size] = total
        for kind in (2, 0, 1):
            go(line(kind, k))
        go(across(0, k))
    for k in range(3):
        for kind in range(3):
            line(kind, k).wait_recv()
            go(across(1 + kind, k))
    for n in range(4):
        for k in range(3):
            across(n, k).wait_recv()

    spread = dot(unp[...], gath[...].reshape(8 * ROWS, 256))
    for e in range(NP + 2):
        for h in range(2):
            src_out[2 * e + h] = spread[e * S:(e + 1) * S, h * 128:h * 128 + 128]
    for copy in started:
        copy.wait_send()


def gather(traces, fir, index):
    dma = pltpu.SemaphoreType.DMA
    return pl.pallas_call(
        gather_kernel,
        in_specs=[
            pl.BlockSpec(memory_space=pltpu.HBM),
            pl.BlockSpec(memory_space=pltpu.HBM),
            pl.BlockSpec(memory_space=pltpu.HBM),
        ],
        out_specs=[pl.BlockSpec(memory_space=pltpu.VMEM)] * 2,
        out_shape=[
            jax.ShapeDtypeStruct((NB + 4, S, 128), F32),
            jax.ShapeDtypeStruct((CHN, T), BF),
        ],
        scratch_shapes=[
            pltpu.SMEM((TAPS,), F32),
            pltpu.SMEM((S,), jnp.int32),
            pltpu.VMEM((CHN, T), F32),
            pltpu.VMEM((2, CHN, 128), F32),
            pltpu.VMEM(((NP + 2) * CHN, 256), BF),
            pltpu.VMEM(((NP + 2) * CHN, 256), BF),
            pltpu.VMEM((7, 256, 256), BF),
            pltpu.VMEM(((NP + 1) * CHN, 256), F32),
            pltpu.VMEM(((NP + 1) * CHN, 256), BF),
            pltpu.VMEM(((NP + 1) * CHN, 256), BF),
            pltpu.VMEM((NP * CHN, 256), BF),
            pltpu.VMEM((4, 48, CHN), BF),
            pltpu.VMEM((2, 16, 256), BF),
            pltpu.VMEM((ROWS, 256), BF),
            pltpu.VMEM((4, ROWS, 256), BF),
            pltpu.VMEM((4, ROWS, 256), BF),
            pltpu.VMEM((8, ROWS, 256), BF),
            pltpu.VMEM(((NP + 2) * S, 8 * ROWS), BF),
            dma((3,)),
            dma((2, 2)),
            dma((2, 2)),
            dma((2, 4, 3, 2)),
            dma((3, 3, 2)),
            dma((4, 3, 2)),
        ],
        compiler_params=pltpu.CompilerParams(
            collective_id=0, has_side_effects=True, vmem_limit_bytes=VA << 20
        ),
        name="gather",
    )(*(pltpu.with_memory_space_constraint(v, pltpu.HBM) for v in (traces, fir, index)))


def corr_kernel(src_ref, nr_ref, o_ref, w_ref, h0, h1):
    g = pl.program_id(0)
    keep = iota((128, 128), 1) > iota((128, 128), 0)

    def build(h, s, half):
        cols = slice(half * 128, half * 128 + 128)

        def turn(b):
            x = src_ref.at[b][pl.ds(s, 128, stride=0), :]
            return pltpu.roll(x, 1, 1, stride=1, stride_axis=0)

        prev = turn(KB)
        for q in range(KB):
            cur = turn(KB - 1 - q)
            h[q * 128:(q + 1) * 128, cols] = jnp.where(keep, prev, cur).astype(BF)
            prev = cur

    @pl.when(g == 0)
    def _():
        w_ref[...] = jnp.zeros_like(w_ref)
        for a in range(4):
            w_ref[a * CHN:(a + 1) * CHN, (3 - a) * 128:(3 - a) * 128 + T] = nr_ref[...]
        for i in range(WIDE):
            build(h0, i, i)

    bufs = (h0, h1)
    for p in range(STEP // WIDE):
        nxt = lax.rem(g * STEP + WIDE * (p + 1), S)
        for i in range(WIDE):
            build(bufs[(p + 1) % 2], nxt + i, i)
        h = bufs[p % 2]
        res = dot(w_ref[:, 256:2048], h[256:2048, :])
        low = dot(w_ref[2 * CHN:, 0:256], h[0:256, :])
        high = dot(w_ref[:3 * CHN, 2048:2304], h[2048:2304, :])
        last = dot(w_ref[:CHN, 2304:], h[2304:, :])
        parts = [res[a * CHN:(a + 1) * CHN] for a in range(4)]
        for a in (2, 3):
            parts[a] += low[(a - 2) * CHN:(a - 1) * CHN]
        for a in (0, 1, 2):
            parts[a] += high[a * CHN:(a + 1) * CHN]
        parts[0] += last
        for a in range(4):
            for i in range(WIDE):
                o_ref[WIDE * p + i, :, a * 128:(a + 1) * 128] = parts[a][
                    :, i * 128:(i + 1) * 128
                ] * (1.0 / math.sqrt(T))


def corr(src_ext, nr):
    return pl.pallas_call(
        corr_kernel,
        grid=(S // STEP,),
        in_specs=[
            pl.BlockSpec(memory_space=pltpu.VMEM),
            pl.BlockSpec(memory_space=pltpu.VMEM),
        ],
        out_specs=pl.BlockSpec((STEP, CHN, 2 * LAG_HALF), lambda g: (g, 0, 0)),
        out_shape=jax.ShapeDtypeStruct((S, CHN, 2 * LAG_HALF), F32),
        scratch_shapes=[
            pltpu.VMEM((4 * CHN, K), BF),
            pltpu.VMEM((K, WIDE * 128), BF),
            pltpu.VMEM((K, WIDE * 128), BF),
        ],
        compiler_params=pltpu.CompilerParams(
            dimension_semantics=("arbitrary",), vmem_limit_bytes=VB << 20
        ),
        name="corr",
    )(src_ext, nr)


def body(traces, fir_taps, source_index):
    src_ext, nr = gather(traces, fir_taps, source_index)
    return corr(src_ext, nr)[None]


def solution(mesh):
    torus = Mesh(mesh.devices.reshape(NZ, NY, NC, NX), AXES)
    chan = AXES[:3]
    return jax.shard_map(
        body,
        mesh=torus,
        in_specs=(P(chan, "tm"), P(), P()),
        out_specs=P("tm", None, chan, None),
        check_vma=False,
    )
```

```python
import math

import jax
import jax.numpy as jnp
from jax import lax
from jax.experimental import pallas as pl
from jax.experimental.pallas import tpu as pltpu
from jax.sharding import Mesh
from jax.sharding import PartitionSpec as P

CHN, T, S = 80, 2048, 64
EPSILON = 1e-05
FIR_HALF, NORM_HALF, LAG_HALF = 32, 64, 256
TAPS = 2 * FIR_HALF + 1
SLOTS = 12
NB = T // 128
NP = T // 256
KB = NB + 3
K = KB * 128
STEP = 16
WIDE = 4
VA, VB = 16, 24
AXES = ("chan_0", "chan_1", "chan_2", "tm")
NZ, NY, NC, NX = 8, 4, 2, 4
CHUNKS = ((0, 48), (48, 48), (96, 32))
UP = (True, False, True)
ROWS = 128
ORDER = (1, 2, 3, 4, 5, 6, 0, 7)
BF = jnp.bfloat16
F32 = jnp.float32


def dot(a, b):
    return jnp.dot(a, b, preferred_element_type=F32)


def dot_t(a, b):
    return lax.dot_general(a, b, (((1,), (1,)), ((), ())), preferred_element_type=F32)


def iota(shape, dim):
    return lax.broadcasted_iota(jnp.int32, shape, dim)


def gather_kernel(
    traces, fir_in, index_in, src_out, nr_out,
    fir, index, xbuf, halo, xh, xl, band, fbuf, fa, fb, nb, pick, edge, pack, zu, zd, gath, unp,
    lsem, hsem, esem, zsem, ysem, csem,
):
    z, y, core, x = (lax.axis_index(a) for a in AXES)
    up_z = {"chan_0": lax.rem(z + 1, NZ)}
    dn_z = {"chan_0": lax.rem(z + NZ - 1, NZ)}
    up2_z = {"chan_0": lax.rem(z + 2, NZ)}
    dn2_z = {"chan_0": lax.rem(z + NZ - 2, NZ)}
    up_y = {"chan_1": lax.rem(y + 1, NY)}
    dn_y = {"chan_1": lax.rem(y + NY - 1, NY)}
    far_y = {"chan_1": lax.rem(y + 2, NY)}
    other = {"chan_2": 1 - core}
    right = {"tm": lax.rem(x + 1, NX)}
    left = {"tm": lax.rem(x + NX - 1, NX)}

    load = pltpu.make_async_copy(traces, xbuf, lsem.at[0])
    load.start()
    taps_load = pltpu.make_async_copy(fir_in, fir, lsem.at[1])
    taps_load.start()
    index_load = pltpu.make_async_copy(index_in, index, lsem.at[2])
    index_load.start()
    barrier = pltpu.get_barrier_semaphore()
    peers = (up2_z, dn2_z, up_z, dn_z, far_y, up_y, dn_y, other, right, left)
    for peer in peers:
        pl.semaphore_signal(barrier, inc=1, device_id=peer, device_id_type=pl.DeviceIdType.MESH)
    pl.semaphore_wait(barrier, len(peers))

    def remote(src, dst, sems, peer):
        return pltpu.make_async_remote_copy(
            src_ref=src, dst_ref=dst, send_sem=sems.at[0], recv_sem=sems.at[1],
            device_id=peer, device_id_type=pl.DeviceIdType.MESH,
        )

    to_right = remote(traces.at[:, T - 128:T], halo.at[0], hsem.at[0], right)
    to_left = remote(traces.at[:, 0:128], halo.at[1], hsem.at[1], left)
    to_right.start()
    to_left.start()

    taps_load.wait()
    index_load.wait()
    lane = iota((8, 128), 1)
    taps = jnp.zeros((8, 128), F32)
    for k in range(TAPS):
        taps = jnp.where(lane == k, fir[TAPS - 1 - k], taps)
    rolled = pltpu.roll(jnp.concatenate([taps] * 16, axis=0), 128 - FIR_HALF, 1, stride=1, stride_axis=0)
    apart = iota((128, 128), 1) - iota((128, 128), 0)
    zero = jnp.zeros((128, 128), F32)
    d1 = jnp.where(apart <= FIR_HALF - 128, rolled, zero)
    d2 = jnp.where(jnp.abs(apart) <= FIR_HALF, rolled, zero)
    d3 = jnp.where(apart >= 128 - FIR_HALF, rolled, zero)
    for n, blocks in enumerate((((d1, zero), (d2, d1)), ((d3, d2), (zero, d3)))):
        for u in range(2):
            for i in range(2):
                whole = blocks[u][i]
                high = whole.astype(BF)
                at = (slice(u * 128, u * 128 + 128), slice(i * 128, i * 128 + 128))
                band[(2 * n,) + at] = high
                band[(2 * n + 1,) + at] = (whole - high.astype(F32)).astype(BF)
    gap = iota((256, 256), 0) - iota((256, 256), 1)
    one = jnp.ones((256, 256), F32)
    none = jnp.zeros((256, 256), F32)
    band[4] = jnp.where((gap >= NORM_HALF) & (gap <= 3 * NORM_HALF), one, none).astype(BF)
    band[5] = jnp.where((gap <= -NORM_HALF) & (gap >= -3 * NORM_HALF), one, none).astype(BF)

    def put(group, half, block):
        high = block.astype(BF)
        at = (slice(group * CHN, group * CHN + CHN), slice(half * 128, half * 128 + 128))
        xh[at] = high
        xl[at] = (block - high.astype(F32)).astype(BF)

    load.wait()
    for b in range(NB):
        put(1 + b // 2, b % 2, xbuf[:, b * 128:b * 128 + 128])
    nothing = jnp.zeros((CHN, 128), F32)
    put(0, 0, nothing)
    put(NP + 1, 1, nothing)

    own = (z * NY + y) * NC + core
    lanes = iota((128, 128), 1)
    subs = iota((128, 128), 0)
    row = jnp.full((8, 128), -1, jnp.int32)
    for s in range(S):
        row = jnp.where(lane == s, index[s], row)
    rows = jnp.concatenate([row] * 16, axis=0)
    inside = (rows >= own * CHN) & (rows < own * CHN + CHN)
    fone, fnone = jnp.ones((128, 128), F32), jnp.zeros((128, 128), F32)
    mine = jnp.where(inside, fone, fnone)
    before = jnp.where(subs < lanes, fone, fnone)
    rank = dot(mine.astype(BF), before.astype(BF))
    hit = jnp.where(inside & (rows == own * CHN + subs), fone, fnone).astype(BF)[0:CHN]
    subf = subs.astype(F32)
    for i in range(4):
        slot = jnp.where(inside & (subf == rank + SLOTS * i), fone, fnone).astype(BF)[0:48]
        pick[i] = dot_t(slot, hit).astype(BF)

    def rows_of(ref, groups):
        return jnp.concatenate([ref[lo * CHN:hi * CHN] for lo, hi in groups], axis=0)

    def after(groups):
        return [(lo + 1, hi + 1) for lo, hi in groups]

    def filtered(groups):
        high = [rows_of(xh, groups), rows_of(xh, after(groups))]
        low = [rows_of(xl, groups), rows_of(xl, after(groups))]
        taken = jnp.concatenate(high + low + high, axis=1)
        return dot(taken, jnp.concatenate([band[n] for n in (0, 2, 0, 2, 1, 3)], axis=0))

    def keep(lo, hi, value):
        n = slice(lo * CHN, hi * CHN)
        fbuf[n] = value
        size = jnp.abs(value)
        high = size.astype(BF)
        fa[n] = high
        fb[n] = (size - high.astype(F32)).astype(BF)

    def normalize(groups):
        taken = [rows_of(ref, part) for ref in (fa, fb) for part in (groups, after(groups))]
        level = dot(
            jnp.concatenate(taken, axis=1),
            jnp.concatenate([band[n] for n in (4, 5, 4, 5)], axis=0),
        )
        below = EPSILON + level / (2 * NORM_HALF + 1)
        at = 0
        for lo, hi in groups:
            size = (hi - lo) * CHN
            first, second = slice(lo * CHN, hi * CHN), slice((lo + 1) * CHN, (hi + 1) * CHN)
            nb[first, 0:128] = (fbuf[first, 128:256] / below[at:at + size, 0:128]).astype(BF)
            nb[first, 128:256] = (fbuf[second, 0:128] / below[at:at + size, 128:256]).astype(BF)
            at += size

    def pair(p):
        return nb[p * CHN:(p + 1) * CHN]

    def fold(j):
        total = dot(pick[0], pair(ORDER[4 * j]))
        for i in range(1, 4):
            total += dot(pick[i], pair(ORDER[4 * j + i]))
        pack[48 * j:48 * j + 48, :] = total.astype(BF)

    def part(ref, k):
        at, size = CHUNKS[k]
        return ref.at[at:at + size]

    def ring(d, far, k):
        slots, two, near = (zu, up2_z, up_z) if d == 0 else (zd, dn2_z, dn_z)
        src = part(pack, k) if far < 2 else part(slots.at[1], k)
        peer = (near, two, near, two)[far]
        return remote(src, part(slots.at[far], k), zsem.at[d, far, k], peer)

    def rings(far, k):
        return [d for d in range(2) if far < 3 or (d == 0) == UP[k]]

    started = [to_right, to_left]

    def go(copy):
        copy.start()
        started.append(copy)

    def send(k):
        for far in (1, 0):
            for d in range(2):
                go(ring(d, far, k))

    keep(1, NP, filtered([(1, NP)]))
    normalize([(1, NP - 1)])
    fold(0)
    send(0)
    to_right.wait_recv()
    to_left.wait_recv()
    put(0, 1, jnp.where(x > 0, halo[0], nothing))
    put(NP + 1, 0, jnp.where(x < NX - 1, halo[1], nothing))
    ends = iota((CHN, 256), 1)
    empty = jnp.zeros((CHN, 256), F32)
    both = filtered([(0, 1), (NP, NP + 1)])
    keep(0, 1, jnp.where((ends >= 128) | (x > 0), both[0:CHN], empty))
    keep(NP, NP + 1, jnp.where((ends < 128) | (x < NX - 1), both[CHN:], empty))
    normalize([(0, 1), (NP - 1, NP)])
    lower = dot(pick[0], pair(0))[0:16]
    upper = dot(pick[0], pair(NP - 1))[0:16]
    edge[0] = jnp.where(x > 0, lower, jnp.zeros_like(lower)).astype(BF)
    edge[1] = jnp.where(x < NX - 1, upper, jnp.zeros_like(upper)).astype(BF)

    edge_left = remote(edge.at[0], pack.at[112:128], esem.at[0], left)
    edge_right = remote(edge.at[1], pack.at[96:112], esem.at[1], right)
    go(edge_left)
    go(edge_right)
    fold(1)
    send(1)
    colsum = jnp.sum(jnp.where(subs == lanes, rows.astype(F32), fnone), axis=1, keepdims=True)
    owner_col = jnp.floor((colsum + 0.5) * (1.0 / CHN))
    owner_row = jnp.floor((rows.astype(F32) + 0.5) * (1.0 / CHN))
    rank_col = jnp.sum(
        jnp.where((owner_row == owner_col) & (lanes < subs), fone, fnone), axis=1, keepdims=True
    )
    residue = owner_col - 8.0 * jnp.floor(owner_col * 0.125)
    line_of = jnp.floor(residue * 0.5)
    other_core = jnp.abs(residue - 2.0 * line_of - core.astype(F32))
    place = ((line_of + NY * other_core) * ROWS + rank_col)[0:S]
    wide = iota((S, 8 * ROWS), 1).astype(F32)
    uone, unone = jnp.ones((S, 8 * ROWS), F32), jnp.zeros((S, 8 * ROWS), F32)
    for e in range(NP + 2):
        offset = 96 if e == 0 else 112 if e == NP + 1 else SLOTS * ORDER.index(e - 1)
        unp[e * S:(e + 1) * S, :] = jnp.where(wide == place + offset, uone, unone).astype(BF)

    band[6] = jnp.where(iota((256, 256), 0) + iota((256, 256), 1) == 255, one, none).astype(BF)
    turned = dot(nb[...], band[6]).astype(BF)
    for p in range(NP):
        nr_out[:, (NP - 1 - p) * 256:(NP - p) * 256] = turned[p * CHN:(p + 1) * CHN]

    def onward(k):
        for d in range(2):
            ring(d, 1, k).wait_recv()
            go(ring(d, 2, k))
            if d in rings(3, k):
                go(ring(d, 3, k))

    onward(0)
    edge_left.wait_recv()
    edge_right.wait_recv()
    send(2)
    onward(1)
    onward(2)

    me = y

    def hold(slot, k):
        at, size = CHUNKS[k]
        return gath.at[slot, at:at + size]

    low, high, far = lax.rem(y + NY - 1, NY), lax.rem(y + 1, NY), lax.rem(y + 2, NY)
    origin = (me, low, high, far)

    def line(kind, k):
        return remote(hold(me, k), hold(me, k), ysem.at[kind, k], (up_y, dn_y, far_y)[kind])

    def across(n, k):
        return remote(hold(origin[n], k), hold(NY + origin[n], k), csem.at[n, k], other)

    for k in range(3):
        at, size = CHUNKS[k]
        total = pack[at:at + size]
        for far in (0, 2, 3):
            for d in rings(far, k):
                ring(d, far, k).wait_recv()
        for far in range(3):
            total += zu[far, at:at + size] + zd[far, at:at + size]
        total += (zu if UP[k] else zd)[3, at:at + size]
        gath[me, at:at + size] = total
        for kind in (2, 0, 1):
            go(line(kind, k))
        go(across(0, k))
    for k in range(3):
        for kind in range(3):
            line(kind, k).wait_recv()
            go(across(1 + kind, k))
    half = NY * ROWS

    def spread(half_of, slots):
        at = half_of * half
        return dot(unp[:, at:at + half], gath[slots].reshape(half, 256))

    near = spread(0, slice(0, NY))
    for e in range(NP + 2):
        for h in range(2):
            src_out[2 * e + h] = near[e * S:(e + 1) * S, h * 128:h * 128 + 128]
    for n in range(4):
        for k in range(3):
            across(n, k).wait_recv()
    rest = spread(1, slice(NY, 2 * NY))
    for e in range(NP + 2):
        for h in range(2):
            src_out[2 * e + h] += rest[e * S:(e + 1) * S, h * 128:h * 128 + 128]
    for copy in started:
        copy.wait_send()


def gather(traces, fir, index):
    dma = pltpu.SemaphoreType.DMA
    return pl.pallas_call(
        gather_kernel,
        in_specs=[
            pl.BlockSpec(memory_space=pltpu.HBM),
            pl.BlockSpec(memory_space=pltpu.HBM),
            pl.BlockSpec(memory_space=pltpu.HBM),
        ],
        out_specs=[pl.BlockSpec(memory_space=pltpu.VMEM)] * 2,
        out_shape=[
            jax.ShapeDtypeStruct((NB + 4, S, 128), F32),
            jax.ShapeDtypeStruct((CHN, T), BF),
        ],
        scratch_shapes=[
            pltpu.SMEM((TAPS,), F32),
            pltpu.SMEM((S,), jnp.int32),
            pltpu.VMEM((CHN, T), F32),
            pltpu.VMEM((2, CHN, 128), F32),
            pltpu.VMEM(((NP + 2) * CHN, 256), BF),
            pltpu.VMEM(((NP + 2) * CHN, 256), BF),
            pltpu.VMEM((7, 256, 256), BF),
            pltpu.VMEM(((NP + 1) * CHN, 256), F32),
            pltpu.VMEM(((NP + 1) * CHN, 256), BF),
            pltpu.VMEM(((NP + 1) * CHN, 256), BF),
            pltpu.VMEM((NP * CHN, 256), BF),
            pltpu.VMEM((4, 48, CHN), BF),
            pltpu.VMEM((2, 16, 256), BF),
            pltpu.VMEM((ROWS, 256), BF),
            pltpu.VMEM((4, ROWS, 256), BF),
            pltpu.VMEM((4, ROWS, 256), BF),
            pltpu.VMEM((8, ROWS, 256), BF),
            pltpu.VMEM(((NP + 2) * S, 8 * ROWS), BF),
            dma((3,)),
            dma((2, 2)),
            dma((2, 2)),
            dma((2, 4, 3, 2)),
            dma((3, 3, 2)),
            dma((4, 3, 2)),
        ],
        compiler_params=pltpu.CompilerParams(
            collective_id=0, has_side_effects=True, vmem_limit_bytes=VA << 20
        ),
        name="gather",
    )(*(pltpu.with_memory_space_constraint(v, pltpu.HBM) for v in (traces, fir, index)))


def corr_kernel(src_ref, nr_ref, o_ref, w_ref, h0, h1):
    g = pl.program_id(0)
    keep = iota((128, 128), 1) > iota((128, 128), 0)

    def build(h, s, half):
        cols = slice(half * 128, half * 128 + 128)

        def turn(b):
            x = src_ref.at[b][pl.ds(s, 128, stride=0), :]
            return pltpu.roll(x, 1, 1, stride=1, stride_axis=0)

        prev = turn(KB)
        for q in range(KB):
            cur = turn(KB - 1 - q)
            h[q * 128:(q + 1) * 128, cols] = jnp.where(keep, prev, cur).astype(BF)
            prev = cur

    @pl.when(g == 0)
    def _():
        w_ref[...] = jnp.zeros_like(w_ref)
        for a in range(4):
            w_ref[a * CHN:(a + 1) * CHN, (3 - a) * 128:(3 - a) * 128 + T] = nr_ref[...]
        for i in range(WIDE):
            build(h0, i, i)

    bufs = (h0, h1)
    for p in range(STEP // WIDE):
        nxt = lax.rem(g * STEP + WIDE * (p + 1), S)
        for i in range(WIDE):
            build(bufs[(p + 1) % 2], nxt + i, i)
        h = bufs[p % 2]
        res = dot(w_ref[:, 256:2048], h[256:2048, :])
        low = dot(w_ref[2 * CHN:, 0:256], h[0:256, :])
        high = dot(w_ref[:3 * CHN, 2048:2304], h[2048:2304, :])
        last = dot(w_ref[:CHN, 2304:], h[2304:, :])
        parts = [res[a * CHN:(a + 1) * CHN] for a in range(4)]
        for a in (2, 3):
            parts[a] += low[(a - 2) * CHN:(a - 1) * CHN]
        for a in (0, 1, 2):
            parts[a] += high[a * CHN:(a + 1) * CHN]
        parts[0] += last
        for a in range(4):
            for i in range(WIDE):
                o_ref[WIDE * p + i, :, a * 128:(a + 1) * 128] = parts[a][
                    :, i * 128:(i + 1) * 128
                ] * (1.0 / math.sqrt(T))


def corr(src_ext, nr):
    return pl.pallas_call(
        corr_kernel,
        grid=(S // STEP,),
        in_specs=[
            pl.BlockSpec(memory_space=pltpu.VMEM),
            pl.BlockSpec(memory_space=pltpu.VMEM),
        ],
        out_specs=pl.BlockSpec((STEP, CHN, 2 * LAG_HALF), lambda g: (g, 0, 0)),
        out_shape=jax.ShapeDtypeStruct((S, CHN, 2 * LAG_HALF), F32),
        scratch_shapes=[
            pltpu.VMEM((4 * CHN, K), BF),
            pltpu.VMEM((K, WIDE * 128), BF),
            pltpu.VMEM((K, WIDE * 128), BF),
        ],
        compiler_params=pltpu.CompilerParams(
            dimension_semantics=("arbitrary",), vmem_limit_bytes=VB << 20
        ),
        name="corr",
    )(src_ext, nr)


def body(traces, fir_taps, source_index):
    src_ext, nr = gather(traces, fir_taps, source_index)
    return corr(src_ext, nr)[None]


def solution(mesh):
    torus = Mesh(mesh.devices.reshape(NZ, NY, NC, NX), AXES)
    chan = AXES[:3]
    return jax.shard_map(
        body,
        mesh=torus,
        in_specs=(P(chan, "tm"), P(), P()),
        out_specs=P("tm", None, chan, None),
        check_vma=False,
    )
```
